256 devices in a mesh: pb: 16 (over z, core), kv: 16 (over y, x).
Axes of the slice: x: 4, y: 4, z: 8, core: 2. Of those that a mesh axis runs over, the one named last changes fastest.
Arguments:
- queries: bfloat16 [393216, 1024], P(('pb', 'kv')), may hold values from -8 to 8
- keys: bfloat16 [524288, 128], P(('kv', 'pb')), may hold values from -6 to 6
- values: bfloat16 [524288, 128], P(('kv', 'pb')), may hold values from -6 to 6
- selected: int32 [6144, 14], P(('pb', 'kv')), may hold values from 1 to 8190, as said below
Outputs:
- attended: bfloat16 [393216, 1024], P(('pb', 'kv'))
The draws below stay inside these ranges and needn't reach their ends.
Inputs may be any that keep to these rules, and one draw needn't show every extreme that they name: `selected`: each row names 14 different blocks, never block 0 or block 8191. Key device k holds blocks k * 32 to (k + 1) * 32 - 1, devices counted with kv slowest; query device d holds query blocks d * 24 to (d + 1) * 24 - 1, devices counted with pb slowest. The query blocks of one device name together at most 2 distinct blocks of one key device, and in every draw some key device has exactly 2 named by every query device.
All inputs are finite; a program needn't handle non-finite values.
Results may differ from the reference program's by a relative error of at most 0.0046.
Values may be sent and summed in bfloat16 or wider, within the bound.
A program may use at most 128 MiB of HBM per device.

```python
import math
import jax
import jax.numpy as jnp
from jax import lax

H = 8
DH = 128
BLOCK = 64
TOPN = 16
QB = 64
TOKENS = 393216
CONTEXT = 524288
NQB = 6144
QBLK_DEV = 24
BLK_DEV = 32
FREE = 14
DEVICES = 256


def draw_queries(key, part):
    own_key = jax.random.fold_in(key, 11)
    return jnp.clip(jax.random.normal(own_key, (TOKENS, H * DH), jnp.float32), -6.0, 6.0).astype(jnp.bfloat16)


def draw_keys(key, part):
    own_key = jax.random.fold_in(key, 13)
    return jnp.clip(jax.random.normal(own_key, (CONTEXT, DH), jnp.float32), -6.0, 6.0).astype(jnp.bfloat16)


def draw_selected(key, part):
    first_key, second_key, order_key, favor_key = jax.random.split(key, 4)
    owners = jnp.arange(DEVICES, dtype=jnp.int32)
    shift_up = (owners == 0).astype(jnp.int32)
    room = BLK_DEV - (owners == 0).astype(jnp.int32) - (owners == DEVICES - 1).astype(jnp.int32)
    first_pick = jax.random.randint(first_key, (DEVICES, DEVICES), 0, 2 ** 20) % room[None, :]
    stride = 1 + jax.random.randint(second_key, (DEVICES, DEVICES), 0, 2 ** 20) % (room[None, :] - 1)
    second_pick = (first_pick + stride) % room[None, :]
    local_ids = jnp.stack([first_pick, second_pick], axis=2) + shift_up[None, :, None]
    candidates = owners[None, :, None] * BLK_DEV + local_ids
    favored = jax.random.randint(favor_key, (), 0, DEVICES)
    order_scores = jax.random.randint(order_key, (DEVICES, DEVICES), 0, 2 ** 20) * DEVICES + owners[None, :]
    order_scores = order_scores + (owners[None, :] == favored).astype(jnp.int32) * 2 ** 29
    ranking = lax.top_k(order_scores, DEVICES)[1].astype(jnp.int32)
    half = FREE // 2
    blocks_all = jnp.arange(NQB, dtype=jnp.int32)
    device_of = blocks_all // QBLK_DEV
    place = ((blocks_all % QBLK_DEV)[:, None] * half + jnp.arange(half, dtype=jnp.int32)[None, :]) % DEVICES
    owner_pick = jnp.take_along_axis(ranking[device_of], place, axis=1)
    pairs = candidates[device_of[:, None], owner_pick]
    return pairs.reshape(NQB, FREE).astype(jnp.int32)


def level_of(stream_key, shape, pieces, low, largest):
    def one(axis_at, parts):
        heights = jax.random.uniform(jax.random.fold_in(jax.random.fold_in(stream_key, 6), axis_at), (parts,), jnp.float32, low / len(pieces), largest / len(pieces))
        return jnp.repeat(jnp.exp(heights), shape[axis_at] // parts).reshape((-1,) + (1,) * (len(shape) - axis_at - 1))

    factor_of = one(*pieces[0])
    for cut in pieces[1:]:
        factor_of = factor_of * one(*cut)
    return factor_of


def normal_values(key, extent, scale, bound, shards=(), kind=jnp.bfloat16):
    entries = jax.random.normal(key, extent, jnp.float32) * scale
    if len(shards) > 0:
        entries = level_of(key, extent, shards, -0.22, 0.18) * entries
    return jnp.clip(entries, min=-bound, max=bound).astype(kind)


def setup_inputs(seed: int = 0) -> dict:
    splits = jax.random.split(jax.random.key(seed), 5)
    queries = draw_queries(jax.random.fold_in(splits[4], 71), 0)
    keys = draw_keys(jax.random.fold_in(splits[4], 71), 0)
    values = normal_values(splits[2], (CONTEXT, DH), 1.0, 6.0, ((0, 256),))
    selected = draw_selected(jax.random.fold_in(splits[4], 71), 0)
    return {"queries": queries, "keys": keys, "values": values, "selected": selected}


def reference(queries, keys, values, selected):
    query_blocks = queries.shape[0] // QB
    block_total = keys.shape[0] // BLOCK
    forced = jnp.broadcast_to(jnp.array([0, block_total - 1], jnp.int32), (query_blocks, 2))
    lists = jnp.concatenate([forced, selected.astype(jnp.int32)], axis=1)
    group_size = math.gcd(query_blocks, 16)
    q_groups = queries.reshape(query_blocks // group_size, group_size, QB * H, DH)
    l_groups = lists.reshape(query_blocks // group_size, group_size, TOPN)
    key_blocks = keys.reshape(block_total, BLOCK, DH)
    value_blocks = values.reshape(block_total, BLOCK, DH)

    def attend(operands):
        q_block, block_ids = operands
        flat_ids = block_ids.reshape(-1)
        k_rows = jnp.take(key_blocks, flat_ids, axis=0).reshape(group_size, TOPN * BLOCK, DH).astype(jnp.float32)
        v_rows = jnp.take(value_blocks, flat_ids, axis=0).reshape(group_size, TOPN * BLOCK, DH).astype(jnp.float32)
        scores = jnp.einsum("gqd,gkd->gqk", q_block.astype(jnp.float32), k_rows) * (DH ** -0.5)
        weights = jnp.exp(scores - jnp.max(scores, axis=-1, keepdims=True))
        totals = jnp.sum(weights, axis=-1, keepdims=True)
        rounded = lax.optimization_barrier(weights.astype(jnp.bfloat16)).astype(jnp.float32)
        weighted = jnp.einsum("gqk,gkd->gqd", rounded, v_rows)
        return (weighted / totals).astype(jnp.bfloat16)

    result = lax.map(attend, (q_groups, l_groups))
    return result.reshape(query_blocks * QB, H * DH)
```

```python
import math

import jax
import jax.numpy as jnp
from jax import lax
from jax.sharding import PartitionSpec as P

H = 8
DH = 128
BLOCK = 64
TOPN = 16
QB = 64
CAP = 2


def holdings(wanted, owner, blocks_here):
    local_ids = owner * blocks_here + jnp.arange(blocks_here, dtype=jnp.int32)
    hits = (wanted[:, None] == local_ids[None, :]).astype(jnp.int32)
    present = jnp.max(hits, axis=0)
    return (present, jnp.cumsum(present) - present)


def slot_lists(present, slot_rank, slots):
    local_ids = jnp.arange(present.shape[-1], dtype=jnp.int32)
    slot_ids = jnp.arange(slots, dtype=jnp.int32)
    matches = (present[..., :, None] == 1) & (slot_rank[..., :, None] == slot_ids)
    return jnp.sum(jnp.where(matches, local_ids[:, None], 0), axis=-2)


def per_device(queries, keys, values, selected):
    pb_count = lax.axis_size("pb")
    kv_count = lax.axis_size("kv")
    devices = pb_count * kv_count
    blocks_here = keys.shape[0] // BLOCK
    query_blocks = queries.shape[0] // QB
    column_blocks = pb_count * blocks_here
    tiles_local = jnp.concatenate(
        [keys.reshape(blocks_here, BLOCK, DH), values.reshape(blocks_here, BLOCK, DH)], axis=2
    )
    column = lax.all_gather(tiles_local, "pb", axis=0, tiled=True)
    slots = CAP
    wanted = selected.reshape(-1)
    owners = jnp.arange(devices, dtype=jnp.int32)
    present, slot_rank = jax.vmap(lambda owner: holdings(wanted, owner, blocks_here))(owners)
    owner_lists = slot_lists(present, slot_rank, slots)
    by_column = owner_lists.reshape(kv_count, pb_count, slots) + (
        jnp.arange(pb_count, dtype=jnp.int32)[None, :, None] * blocks_here
    )
    by_column = by_column.reshape(kv_count, pb_count * slots)
    asked_for = lax.all_to_all(by_column, "kv", split_axis=0, concat_axis=0, tiled=True)
    outgoing = jnp.take(column, asked_for.reshape(-1), axis=0).reshape(
        kv_count, pb_count * slots, BLOCK, 2 * DH
    )
    fetched = lax.all_to_all(outgoing, "kv", split_axis=0, concat_axis=0, tiled=True)
    tile_table = fetched.reshape(devices * slots, BLOCK, 2 * DH)
    owner_of = selected // blocks_here
    positions = owner_of * slots + jnp.take(slot_rank.reshape(-1), selected)
    me_kv = lax.axis_index("kv")
    ends = jnp.concatenate([column[:1], column[column_blocks - 1 :]], axis=0)
    ends = jnp.where(
        jnp.stack([me_kv == 0, me_kv == kv_count - 1])[:, None, None], ends, jnp.zeros_like(ends)
    )
    ends = lax.psum(ends, "kv")
    tile_table = jnp.concatenate([tile_table, ends], axis=0)
    extra_base = devices * slots
    leading_positions = jnp.broadcast_to(
        jnp.array([extra_base, extra_base + 1], jnp.int32), (query_blocks, 2)
    )
    positions = jnp.concatenate([leading_positions, positions], axis=1)
    group_size = math.gcd(query_blocks, 8)
    q_groups = queries.reshape(query_blocks // group_size, group_size, QB * H, DH)
    p_groups = positions.reshape(query_blocks // group_size, group_size, TOPN)

    def attend(operands):
        q_block, positions_in = operands
        gathered = jnp.take(tile_table, positions_in.reshape(-1), axis=0).reshape(
            group_size, TOPN * BLOCK, 2 * DH
        )
        scores = jnp.einsum(
            "gqd,gkd->gqk", q_block, gathered[..., :DH], preferred_element_type=jnp.float32
        ) * DH ** (-0.5)
        weights = jnp.exp(scores - jnp.max(scores, axis=-1, keepdims=True))
        totals = jnp.sum(weights, axis=-1, keepdims=True)
        weighted = jnp.einsum(
            "gqk,gkd->gqd",
            weights.astype(jnp.bfloat16),
            gathered[..., DH:],
            preferred_element_type=jnp.float32,
        )
        return (weighted / totals).astype(jnp.bfloat16)

    result = lax.map(attend, (q_groups, p_groups))
    return result.reshape(query_blocks * QB, H * DH)


def solution(mesh):
    placed = (
        P(("pb", "kv"), None),
        P(("kv", "pb"), None),
        P(("kv", "pb"), None),
        P(("pb", "kv"), None),
    )
    return jax.shard_map(
        per_device, mesh=mesh, in_specs=placed, out_specs=P(("pb", "kv"), None), check_vma=False
    )
```

```python
import math

import jax
import jax.numpy as jnp
from jax import lax
from jax.sharding import PartitionSpec as P

H = 8
DH = 128
BLOCK = 64
TOPN = 16
QB = 64
CAP = 2


def holdings(wanted, owner, blocks_here):
    local_ids = owner * blocks_here + jnp.arange(blocks_here, dtype=jnp.int32)
    hits = (wanted[:, None] == local_ids[None, :]).astype(jnp.int32)
    present = jnp.max(hits, axis=0)
    return (present, jnp.cumsum(present) - present)


def slot_lists(present, slot_rank, slots):
    local_ids = jnp.arange(present.shape[-1], dtype=jnp.int32)
    slot_ids = jnp.arange(slots, dtype=jnp.int32)
    matches = (present[..., :, None] == 1) & (slot_rank[..., :, None] == slot_ids)
    return jnp.sum(jnp.where(matches, local_ids[:, None], 0), axis=-2)


def per_device(queries, keys, values, selected):
    pb_count = lax.axis_size("pb")
    kv_count = lax.axis_size("kv")
    devices = pb_count * kv_count
    blocks_here = keys.shape[0] // BLOCK
    query_blocks = queries.shape[0] // QB
    column_blocks = pb_count * blocks_here
    tiles_local = jnp.concatenate(
        [keys.reshape(blocks_here, BLOCK, DH), values.reshape(blocks_here, BLOCK, DH)], axis=2
    )
    column = lax.all_gather(tiles_local, "pb", axis=0, tiled=True)
    slots = CAP
    wanted = selected.reshape(-1)
    owners = jnp.arange(devices, dtype=jnp.int32)
    present, slot_rank = jax.vmap(lambda owner: holdings(wanted, owner, blocks_here))(owners)
    owner_lists = slot_lists(present, slot_rank, slots)
    by_column = owner_lists.reshape(kv_count, pb_count, slots) + (
        jnp.arange(pb_count, dtype=jnp.int32)[None, :, None] * blocks_here
    )
    by_column = by_column.reshape(kv_count, pb_count * slots)
    asked_for = lax.all_to_all(by_column, "kv", split_axis=0, concat_axis=0, tiled=True)
    me_kv = lax.axis_index("kv")
    end_pick = jnp.where(me_kv == kv_count - 1, column_blocks - 1, 0).astype(jnp.int32)
    picks = jnp.concatenate(
        [asked_for.reshape(kv_count, pb_count * slots), jnp.broadcast_to(end_pick, (kv_count, 1))], axis=1
    )
    outgoing = jnp.take(column, picks.reshape(-1), axis=0).reshape(
        kv_count, pb_count * slots + 1, BLOCK, 2 * DH
    )
    fetched = lax.all_to_all(outgoing, "kv", split_axis=0, concat_axis=0, tiled=True)
    tile_table = fetched.reshape(devices * slots + kv_count, BLOCK, 2 * DH)
    owner_of = selected // blocks_here
    positions = owner_of * slots + jnp.take(slot_rank.reshape(-1), selected)
    positions = positions + owner_of // pb_count
    row = pb_count * slots + 1
    leading_positions = jnp.broadcast_to(
        jnp.array([row - 1, kv_count * row - 1], jnp.int32), (query_blocks, 2)
    )
    positions = jnp.concatenate([leading_positions, positions], axis=1)
    group_size = math.gcd(query_blocks, 8)
    q_groups = queries.reshape(query_blocks // group_size, group_size, QB * H, DH)
    p_groups = positions.reshape(query_blocks // group_size, group_size, TOPN)

    def attend(operands):
        q_block, positions_in = operands
        gathered = jnp.take(tile_table, positions_in.reshape(-1), axis=0).reshape(
            group_size, TOPN * BLOCK, 2 * DH
        )
        scores = jnp.einsum(
            "gqd,gkd->gqk", q_block, gathered[..., :DH], preferred_element_type=jnp.float32
        ) * DH ** (-0.5)
        weights = jnp.exp(scores - jnp.max(scores, axis=-1, keepdims=True))
        totals = jnp.sum(weights, axis=-1, keepdims=True)
        weighted = jnp.einsum(
            "gqk,gkd->gqd",
            weights.astype(jnp.bfloat16),
            gathered[..., DH:],
            preferred_element_type=jnp.float32,
        )
        return (weighted / totals).astype(jnp.bfloat16)

    result = lax.map(attend, (q_groups, p_groups))
    return result.reshape(query_blocks * QB, H * DH)


def solution(mesh):
    placed = (
        P(("pb", "kv"), None),
        P(("kv", "pb"), None),
        P(("kv", "pb"), None),
        P(("pb", "kv"), None),
    )
    return jax.shard_map(
        per_device, mesh=mesh, in_specs=placed, out_specs=P(("pb", "kv"), None), check_vma=False
    )
```

```python
import math

import jax
import jax.numpy as jnp
from jax import lax
from jax.experimental import pallas as pl
from jax.experimental.pallas import tpu as pltpu
from jax.sharding import PartitionSpec as P

H = 8
DH = 128
BLOCK = 64
TOPN = 16
QB = 64
CAP = 2


def holdings(wanted, owner, blocks_here):
    local_ids = owner * blocks_here + jnp.arange(blocks_here, dtype=jnp.int32)
    hits = (wanted[:, None] == local_ids[None, :]).astype(jnp.int32)
    present = jnp.max(hits, axis=0)
    return (present, jnp.cumsum(present) - present)


def slot_lists(present, slot_rank, slots):
    local_ids = jnp.arange(present.shape[-1], dtype=jnp.int32)
    slot_ids = jnp.arange(slots, dtype=jnp.int32)
    matches = (present[..., :, None] == 1) & (slot_rank[..., :, None] == slot_ids)
    return jnp.sum(jnp.where(matches, local_ids[:, None], 0), axis=-2)


def per_device(queries, keys, values, selected):
    pb_count = lax.axis_size("pb")
    kv_count = lax.axis_size("kv")
    devices = pb_count * kv_count
    blocks_here = keys.shape[0] // BLOCK
    query_blocks = queries.shape[0] // QB
    column_blocks = pb_count * blocks_here
    tiles_local = jnp.concatenate(
        [keys.reshape(blocks_here, BLOCK, DH), values.reshape(blocks_here, BLOCK, DH)], axis=2
    )
    column = lax.all_gather(tiles_local, "pb", axis=0, tiled=True)
    slots = CAP
    wanted = selected.reshape(-1)
    owners = jnp.arange(devices, dtype=jnp.int32)
    present, slot_rank = jax.vmap(lambda owner: holdings(wanted, owner, blocks_here))(owners)
    owner_lists = slot_lists(present, slot_rank, slots)
    by_column = owner_lists.reshape(kv_count, pb_count, slots) + (
        jnp.arange(pb_count, dtype=jnp.int32)[None, :, None] * blocks_here
    )
    by_column = by_column.reshape(kv_count, pb_count * slots)
    asked_for = lax.all_to_all(by_column, "kv", split_axis=0, concat_axis=0, tiled=True)
    me_kv = lax.axis_index("kv")
    end_pick = jnp.where(me_kv == kv_count - 1, column_blocks - 1, 0).astype(jnp.int32)
    picks = jnp.concatenate(
        [asked_for.reshape(kv_count, pb_count * slots), jnp.broadcast_to(end_pick, (kv_count, 1))], axis=1
    )
    outgoing = jnp.take(column, picks.reshape(-1), axis=0, mode="clip").reshape(
        kv_count, pb_count * slots + 1, BLOCK, 2 * DH
    )
    fetched = lax.all_to_all(outgoing, "kv", split_axis=0, concat_axis=0, tiled=True)
    tile_table = fetched.reshape(devices * slots + kv_count, BLOCK, 2 * DH)
    owner_of = selected // blocks_here
    positions = owner_of * slots + jnp.take(slot_rank.reshape(-1), selected)
    positions = positions + owner_of // pb_count
    row = pb_count * slots + 1
    leading_positions = jnp.broadcast_to(
        jnp.array([row - 1, kv_count * row - 1], jnp.int32), (query_blocks, 2)
    )
    positions = jnp.concatenate([leading_positions, positions], axis=1)
    positions = jnp.clip(positions, 0, tile_table.shape[0] - 1).reshape(-1)
    return attend_blocks(queries, tile_table, positions)


HEAD_GROUP = 4


def attend_kernel(pos_ref, q_ref, table_hbm, o_ref, kvbuf, sems):
    step = pl.program_id(0)
    steps = pl.num_programs(0)

    def fetch(block, slot):
        for j in range(TOPN):
            pltpu.make_async_copy(
                table_hbm.at[pos_ref[block * TOPN + j]], kvbuf.at[slot, j], sems.at[slot, j]
            ).start()

    @pl.when(step == 0)
    def _():
        fetch(0, 0)

    slot = step % 2

    @pl.when(step + 1 < steps)
    def _():
        fetch(step + 1, 1 - slot)

    for j in range(TOPN):
        pltpu.make_async_copy(table_hbm.at[0], kvbuf.at[slot, j], sems.at[slot, j]).wait()
    tiles = kvbuf[slot]
    k_rows = tiles[:, :, :DH].reshape(TOPN * BLOCK, DH)
    v_rows = tiles[:, :, DH:].reshape(TOPN * BLOCK, DH)
    for g in range(H // HEAD_GROUP):
        heads = range(g * HEAD_GROUP, (g + 1) * HEAD_GROUP)
        q_rows = jnp.concatenate([q_ref[:, h * DH : (h + 1) * DH] for h in heads], axis=0)
        scores = lax.dot_general(
            q_rows, k_rows, (((1,), (1,)), ((), ())), preferred_element_type=jnp.float32
        ) * DH ** (-0.5)
        weights = jnp.exp(scores - jnp.max(scores, axis=-1, keepdims=True))
        totals = jnp.sum(weights, axis=-1, keepdims=True)
        weighted = jnp.dot(
            weights.astype(jnp.bfloat16), v_rows, preferred_element_type=jnp.float32
        )
        out = (weighted / totals).astype(o_ref.dtype)
        for i, h in enumerate(heads):
            o_ref[:, h * DH : (h + 1) * DH] = out[i * QB : (i + 1) * QB]


def attend_blocks(queries, tile_table, positions):
    query_blocks = queries.shape[0] // QB
    return pl.pallas_call(
        attend_kernel,
        out_shape=jax.ShapeDtypeStruct(queries.shape, queries.dtype),
        grid_spec=pltpu.PrefetchScalarGridSpec(
            num_scalar_prefetch=1,
            grid=(query_blocks,),
            in_specs=[
                pl.BlockSpec((QB, H * DH), lambda i, pos: (i, 0)),
                pl.BlockSpec(memory_space=pl.ANY),
            ],
            out_specs=pl.BlockSpec((QB, H * DH), lambda i, pos: (i, 0)),
            scratch_shapes=[
                pltpu.VMEM((2, TOPN, BLOCK, 2 * DH), tile_table.dtype),
                pltpu.SemaphoreType.DMA((2, TOPN)),
            ],
        ),
        compiler_params=pltpu.CompilerParams(dimension_semantics=("arbitrary",)),
        cost_estimate=pl.CostEstimate(
            flops=4 * queries.shape[0] * H * TOPN * BLOCK * DH,
            transcendentals=queries.shape[0] * H * TOPN * BLOCK,
            bytes_accessed=2 * queries.size * 2 + query_blocks * TOPN * BLOCK * 2 * DH * 2,
        ),
    )(positions, queries, tile_table)


def solution(mesh):
    placed = (
        P(("pb", "kv"), None),
        P(("kv", "pb"), None),
        P(("kv", "pb"), None),
        P(("pb", "kv"), None),
    )
    return jax.shard_map(
        per_device, mesh=mesh, in_specs=placed, out_specs=P(("pb", "kv"), None), check_vma=False
    )
```

```python
import math

import jax
import jax.numpy as jnp
from jax import lax
from jax.experimental import pallas as pl
from jax.experimental.pallas import tpu as pltpu
from jax.sharding import PartitionSpec as P

H = 8
DH = 128
BLOCK = 64
TOPN = 16
QB = 64
CAP = 2


def holdings(wanted, owner, blocks_here):
    local_ids = owner * blocks_here + jnp.arange(blocks_here, dtype=jnp.int32)
    hits = (wanted[:, None] == local_ids[None, :]).astype(jnp.int32)
    present = jnp.max(hits, axis=0)
    return (present, jnp.cumsum(present) - present)


def slot_lists(present, slot_rank, slots):
    local_ids = jnp.arange(present.shape[-1], dtype=jnp.int32)
    slot_ids = jnp.arange(slots, dtype=jnp.int32)
    matches = (present[..., :, None] == 1) & (slot_rank[..., :, None] == slot_ids)
    return jnp.sum(jnp.where(matches, local_ids[:, None], 0), axis=-2)


def per_device(queries, keys, values, selected):
    pb_count = lax.axis_size("pb")
    kv_count = lax.axis_size("kv")
    devices = pb_count * kv_count
    blocks_here = keys.shape[0] // BLOCK
    query_blocks = queries.shape[0] // QB
    column_blocks = pb_count * blocks_here
    tiles_local = jnp.concatenate(
        [keys.reshape(blocks_here, BLOCK, DH), values.reshape(blocks_here, BLOCK, DH)], axis=2
    )
    column = lax.all_gather(tiles_local, "pb", axis=0, tiled=True)
    slots = CAP
    wanted = selected.reshape(-1)
    owners = jnp.arange(devices, dtype=jnp.int32)
    present, slot_rank = jax.vmap(lambda owner: holdings(wanted, owner, blocks_here))(owners)
    owner_lists = slot_lists(present, slot_rank, slots)
    by_column = owner_lists.reshape(kv_count, pb_count, slots) + (
        jnp.arange(pb_count, dtype=jnp.int32)[None, :, None] * blocks_here
    )
    by_column = by_column.reshape(kv_count, pb_count * slots)
    asked_for = lax.all_to_all(by_column, "kv", split_axis=0, concat_axis=0, tiled=True)
    me_kv = lax.axis_index("kv")
    end_pick = jnp.where(me_kv == kv_count - 1, column_blocks - 1, 0).astype(jnp.int32)
    picks = jnp.concatenate(
        [asked_for.reshape(kv_count, pb_count * slots), jnp.broadcast_to(end_pick, (kv_count, 1))], axis=1
    )
    outgoing = jnp.take(column, picks.reshape(-1), axis=0, mode="clip").reshape(
        kv_count, pb_count * slots + 1, BLOCK, 2 * DH
    )
    fetched = exchange(outgoing)
    tile_table = fetched.reshape(devices * slots + kv_count, BLOCK, 2 * DH)
    owner_of = selected // blocks_here
    positions = owner_of * slots + jnp.take(slot_rank.reshape(-1), selected)
    positions = positions + owner_of // pb_count
    row = pb_count * slots + 1
    leading_positions = jnp.broadcast_to(
        jnp.array([row - 1, kv_count * row - 1], jnp.int32), (query_blocks, 2)
    )
    positions = jnp.concatenate([leading_positions, positions], axis=1)
    positions = jnp.clip(positions, 0, tile_table.shape[0] - 1).reshape(-1)
    return attend_blocks(queries, tile_table, positions)


HEAD_GROUP = 4


def exchange_kernel(out_hbm, fetched_hbm, send_sems, recv_sems, local_sem):
    n = out_hbm.shape[0]
    me = lax.axis_index("kv")
    row = lax.axis_index("pb")
    barrier = pltpu.get_barrier_semaphore()
    for r in range(1, n):
        pl.semaphore_signal(
            barrier, inc=1, device_id=(row, lax.rem(me + r, n)), device_id_type=pl.DeviceIdType.MESH
        )
    pl.semaphore_wait(barrier, n - 1)
    local = pltpu.make_async_copy(out_hbm.at[me], fetched_hbm.at[me], local_sem)
    local.start()
    sends = []
    for r in range(1, n):
        peer = lax.rem(me + r, n)
        copy = pltpu.make_async_remote_copy(
            src_ref=out_hbm.at[peer],
            dst_ref=fetched_hbm.at[me],
            send_sem=send_sems.at[r],
            recv_sem=recv_sems.at[r],
            device_id=(row, peer),
            device_id_type=pl.DeviceIdType.MESH,
        )
        copy.start()
        sends.append(copy)
    for copy in sends:
        copy.wait_send()
    for r in range(1, n):
        source = lax.rem(me + n - r, n)
        pltpu.make_async_remote_copy(
            src_ref=out_hbm.at[source],
            dst_ref=fetched_hbm.at[source],
            send_sem=send_sems.at[r],
            recv_sem=recv_sems.at[r],
            device_id=(row, source),
            device_id_type=pl.DeviceIdType.MESH,
        ).wait_recv()
    local.wait()


def exchange(outgoing):
    n = outgoing.shape[0]
    return pl.pallas_call(
        exchange_kernel,
        out_shape=jax.ShapeDtypeStruct(outgoing.shape, outgoing.dtype),
        in_specs=[pl.BlockSpec(memory_space=pl.ANY)],
        out_specs=pl.BlockSpec(memory_space=pl.ANY),
        scratch_shapes=[
            pltpu.SemaphoreType.DMA((n,)),
            pltpu.SemaphoreType.DMA((n,)),
            pltpu.SemaphoreType.DMA(()),
        ],
        compiler_params=pltpu.CompilerParams(collective_id=0, has_side_effects=True),
    )(outgoing)


def attend_kernel(pos_ref, q_ref, table_hbm, o_ref, kvbuf, sems):
    step = pl.program_id(0)
    steps = pl.num_programs(0)

    def fetch(block, slot):
        for j in range(TOPN):
            pltpu.make_async_copy(
                table_hbm.at[pos_ref[block * TOPN + j]], kvbuf.at[slot, j], sems.at[slot, j]
            ).start()

    @pl.when(step == 0)
    def _():
        fetch(0, 0)

    slot = step % 2

    @pl.when(step + 1 < steps)
    def _():
        fetch(step + 1, 1 - slot)

    for j in range(TOPN):
        pltpu.make_async_copy(table_hbm.at[0], kvbuf.at[slot, j], sems.at[slot, j]).wait()
    tiles = kvbuf[slot]
    k_rows = tiles[:, :, :DH].reshape(TOPN * BLOCK, DH)
    v_rows = tiles[:, :, DH:].reshape(TOPN * BLOCK, DH)
    for g in range(H // HEAD_GROUP):
        heads = range(g * HEAD_GROUP, (g + 1) * HEAD_GROUP)
        q_rows = jnp.concatenate([q_ref[:, h * DH : (h + 1) * DH] for h in heads], axis=0)
        scores = lax.dot_general(
            q_rows, k_rows, (((1,), (1,)), ((), ())), preferred_element_type=jnp.float32
        ) * DH ** (-0.5)
        weights = jnp.exp(scores - jnp.max(scores, axis=-1, keepdims=True))
        totals = jnp.sum(weights, axis=-1, keepdims=True)
        weighted = jnp.dot(
            weights.astype(jnp.bfloat16), v_rows, preferred_element_type=jnp.float32
        )
        out = (weighted / totals).astype(o_ref.dtype)
        for i, h in enumerate(heads):
            o_ref[:, h * DH : (h + 1) * DH] = out[i * QB : (i + 1) * QB]


def attend_blocks(queries, tile_table, positions):
    query_blocks = queries.shape[0] // QB
    return pl.pallas_call(
        attend_kernel,
        out_shape=jax.ShapeDtypeStruct(queries.shape, queries.dtype),
        grid_spec=pltpu.PrefetchScalarGridSpec(
            num_scalar_prefetch=1,
            grid=(query_blocks,),
            in_specs=[
                pl.BlockSpec((QB, H * DH), lambda i, pos: (i, 0)),
                pl.BlockSpec(memory_space=pl.ANY),
            ],
            out_specs=pl.BlockSpec((QB, H * DH), lambda i, pos: (i, 0)),
            scratch_shapes=[
                pltpu.VMEM((2, TOPN, BLOCK, 2 * DH), tile_table.dtype),
                pltpu.SemaphoreType.DMA((2, TOPN)),
            ],
        ),
        compiler_params=pltpu.CompilerParams(dimension_semantics=("arbitrary",)),
        cost_estimate=pl.CostEstimate(
            flops=4 * queries.shape[0] * H * TOPN * BLOCK * DH,
            transcendentals=queries.shape[0] * H * TOPN * BLOCK,
            bytes_accessed=2 * queries.size * 2 + query_blocks * TOPN * BLOCK * 2 * DH * 2,
        ),
    )(positions, queries, tile_table)


def solution(mesh):
    placed = (
        P(("pb", "kv"), None),
        P(("kv", "pb"), None),
        P(("kv", "pb"), None),
        P(("pb", "kv"), None),
    )
    return jax.shard_map(
        per_device, mesh=mesh, in_specs=placed, out_specs=P(("pb", "kv"), None), check_vma=False
    )
```

```python
import math

import jax
import jax.numpy as jnp
from jax import lax
from jax.experimental import pallas as pl
from jax.experimental.pallas import tpu as pltpu
from jax.sharding import PartitionSpec as P

H = 8
DH = 128
BLOCK = 64
TOPN = 16
QB = 64
CAP = 2


def holdings(wanted, owner, blocks_here):
    local_ids = owner * blocks_here + jnp.arange(blocks_here, dtype=jnp.int32)
    hits = (wanted[:, None] == local_ids[None, :]).astype(jnp.int32)
    present = jnp.max(hits, axis=0)
    return (present, jnp.cumsum(present) - present)


def slot_lists(present, slot_rank, slots):
    local_ids = jnp.arange(present.shape[-1], dtype=jnp.int32)
    slot_ids = jnp.arange(slots, dtype=jnp.int32)
    matches = (present[..., :, None] == 1) & (slot_rank[..., :, None] == slot_ids)
    return jnp.sum(jnp.where(matches, local_ids[:, None], 0), axis=-2)


def per_device(queries, keys, values, selected):
    pb_count = lax.axis_size("pb")
    kv_count = lax.axis_size("kv")
    devices = pb_count * kv_count
    blocks_here = keys.shape[0] // BLOCK
    query_blocks = queries.shape[0] // QB
    column_blocks = pb_count * blocks_here
    tiles_local = jnp.concatenate(
        [keys.reshape(blocks_here, BLOCK, DH), values.reshape(blocks_here, BLOCK, DH)], axis=2
    )
    column = lax.all_gather(tiles_local, "pb", axis=0, tiled=True)
    slots = CAP
    wanted = selected.reshape(-1)
    owners = jnp.arange(devices, dtype=jnp.int32)
    present, slot_rank = jax.vmap(lambda owner: holdings(wanted, owner, blocks_here))(owners)
    owner_lists = slot_lists(present, slot_rank, slots)
    by_column = owner_lists.reshape(kv_count, pb_count, slots) + (
        jnp.arange(pb_count, dtype=jnp.int32)[None, :, None] * blocks_here
    )
    by_column = by_column.reshape(kv_count, pb_count * slots)
    asked_for = lax.all_to_all(by_column, "kv", split_axis=0, concat_axis=0, tiled=True)
    me_kv = lax.axis_index("kv")
    end_pick = jnp.where(me_kv == kv_count - 1, column_blocks - 1, 0).astype(jnp.int32)
    picks = jnp.concatenate(
        [asked_for.reshape(kv_count, pb_count * slots), jnp.broadcast_to(end_pick, (kv_count, 1))], axis=1
    )
    outgoing = jnp.take(column, picks.reshape(-1), axis=0, mode="clip").reshape(
        kv_count, pb_count * slots + 1, BLOCK, 2 * DH
    )
    fetched = exchange(outgoing)
    tile_table = fetched.reshape(devices * slots + kv_count, BLOCK, 2 * DH)
    owner_of = selected // blocks_here
    positions = owner_of * slots + jnp.take(slot_rank.reshape(-1), selected)
    positions = positions + owner_of // pb_count
    row = pb_count * slots + 1
    leading_positions = jnp.broadcast_to(
        jnp.array([row - 1, kv_count * row - 1], jnp.int32), (query_blocks, 2)
    )
    positions = jnp.concatenate([leading_positions, positions], axis=1)
    positions = jnp.clip(positions, 0, tile_table.shape[0] - 1).reshape(-1)
    return attend_blocks(queries, tile_table, positions)


HEAD_GROUP = 4


SIDE = 4
STEPS = [(dx, dy) for dy in range(SIDE) for dx in range(SIDE) if (dx, dy) != (0, 0)]
DIRECT = [(dx, dy) for (dx, dy) in STEPS if dx != SIDE // 2 and dy != SIDE // 2]
FAR = [(dx, dy) for (dx, dy) in STEPS if dx == SIDE // 2 or dy == SIDE // 2]


def relays_of(dx, dy):
    if dx == SIDE // 2 and dy == SIDE // 2:
        return [(-1, -1), (1, 1)]
    if dx == SIDE // 2:
        return [(-1, 0), (1, 0)]
    return [(0, -1), (0, 1)]


def exchange_kernel(out_hbm, fetched_hbm, relay_hbm, d_send, d_recv, r_send, r_recv, f_send, f_recv, local_sem):
    rows = out_hbm.shape[1]
    parts = [(0, rows // 2), (rows // 2, rows - rows // 2)]
    me = lax.axis_index("kv")
    line = lax.axis_index("pb")
    mx = me % SIDE
    my = me // SIDE

    def at(dx, dy):
        return ((my + dy + SIDE) % SIDE) * SIDE + (mx + dx + SIDE) % SIDE

    def remote(src, dst, send, recv, target):
        return pltpu.make_async_remote_copy(
            src_ref=src, dst_ref=dst, send_sem=send, recv_sem=recv,
            device_id=(line, target), device_id_type=pl.DeviceIdType.MESH,
        )

    barrier = pltpu.get_barrier_semaphore()
    for dx, dy in STEPS:
        pl.semaphore_signal(
            barrier, inc=1, device_id=(line, at(dx, dy)), device_id_type=pl.DeviceIdType.MESH
        )
    pl.semaphore_wait(barrier, len(STEPS))
    local = pltpu.make_async_copy(out_hbm.at[me], fetched_hbm.at[me], local_sem)
    local.start()
    sent = []
    for t, (dx, dy) in enumerate(FAR):
        for h, (rx, ry) in enumerate(relays_of(dx, dy)):
            f = 2 * t + h
            lo, size = parts[h]
            copy = remote(
                out_hbm.at[at(dx, dy), pl.ds(lo, size)], relay_hbm.at[f, pl.ds(0, size)],
                r_send.at[f], r_recv.at[f], at(rx, ry),
            )
            copy.start()
            sent.append(copy)
    for dx, dy in DIRECT:
        k = dy * SIDE + dx
        copy = remote(out_hbm.at[at(dx, dy)], fetched_hbm.at[me], d_send.at[k], d_recv.at[k], at(dx, dy))
        copy.start()
        sent.append(copy)
    for t, (dx, dy) in enumerate(FAR):
        for h, (rx, ry) in enumerate(relays_of(dx, dy)):
            f = 2 * t + h
            lo, size = parts[h]
            held = relay_hbm.at[f, pl.ds(0, size)]
            remote(held, held, r_send.at[f], r_recv.at[f], at(-rx, -ry)).wait_recv()
            copy = remote(
                held, fetched_hbm.at[at(-rx, -ry), pl.ds(lo, size)],
                f_send.at[f], f_recv.at[f], at(dx - rx, dy - ry),
            )
            copy.start()
            sent.append(copy)
    for copy in sent:
        copy.wait_send()
    for dx, dy in DIRECT:
        k = dy * SIDE + dx
        source = at(-dx, -dy)
        remote(
            out_hbm.at[source], fetched_hbm.at[source], d_send.at[k], d_recv.at[k], source
        ).wait_recv()
    for t, (dx, dy) in enumerate(FAR):
        for h in range(2):
            f = 2 * t + h
            lo, size = parts[h]
            source = at(-dx, -dy)
            part = fetched_hbm.at[source, pl.ds(lo, size)]
            remote(part, part, f_send.at[f], f_recv.at[f], source).wait_recv()
    local.wait()


def exchange(outgoing):
    n, rows = outgoing.shape[:2]
    flows = 2 * len(FAR)
    fetched, _ = pl.pallas_call(
        exchange_kernel,
        out_shape=(
            jax.ShapeDtypeStruct(outgoing.shape, outgoing.dtype),
            jax.ShapeDtypeStruct((flows, rows - rows // 2) + outgoing.shape[2:], outgoing.dtype),
        ),
        in_specs=[pl.BlockSpec(memory_space=pl.ANY)],
        out_specs=(pl.BlockSpec(memory_space=pl.ANY), pl.BlockSpec(memory_space=pl.ANY)),
        scratch_shapes=[
            pltpu.SemaphoreType.DMA((n,)),
            pltpu.SemaphoreType.DMA((n,)),
            pltpu.SemaphoreType.DMA((flows,)),
            pltpu.SemaphoreType.DMA((flows,)),
            pltpu.SemaphoreType.DMA((flows,)),
            pltpu.SemaphoreType.DMA((flows,)),
            pltpu.SemaphoreType.DMA(()),
        ],
        compiler_params=pltpu.CompilerParams(collective_id=0, has_side_effects=True),
    )(outgoing)
    return fetched


def attend_kernel(pos_ref, q_ref, table_hbm, o_ref, kvbuf, sems):
    step = pl.program_id(0)
    steps = pl.num_programs(0)

    def fetch(block, slot):
        for j in range(TOPN):
            pltpu.make_async_copy(
                table_hbm.at[pos_ref[block * TOPN + j]], kvbuf.at[slot, j], sems.at[slot, j]
            ).start()

    @pl.when(step == 0)
    def _():
        fetch(0, 0)

    slot = step % 2

    @pl.when(step + 1 < steps)
    def _():
        fetch(step + 1, 1 - slot)

    for j in range(TOPN):
        pltpu.make_async_copy(table_hbm.at[0], kvbuf.at[slot, j], sems.at[slot, j]).wait()
    tiles = kvbuf[slot]
    k_rows = tiles[:, :, :DH].reshape(TOPN * BLOCK, DH)
    v_rows = tiles[:, :, DH:].reshape(TOPN * BLOCK, DH)
    for g in range(H // HEAD_GROUP):
        heads = range(g * HEAD_GROUP, (g + 1) * HEAD_GROUP)
        q_rows = jnp.concatenate([q_ref[:, h * DH : (h + 1) * DH] for h in heads], axis=0)
        scores = lax.dot_general(
            q_rows, k_rows, (((1,), (1,)), ((), ())), preferred_element_type=jnp.float32
        ) * DH ** (-0.5)
        weights = jnp.exp(scores - jnp.max(scores, axis=-1, keepdims=True))
        totals = jnp.sum(weights, axis=-1, keepdims=True)
        weighted = jnp.dot(
            weights.astype(jnp.bfloat16), v_rows, preferred_element_type=jnp.float32
        )
        out = (weighted / totals).astype(o_ref.dtype)
        for i, h in enumerate(heads):
            o_ref[:, h * DH : (h + 1) * DH] = out[i * QB : (i + 1) * QB]


def attend_blocks(queries, tile_table, positions):
    query_blocks = queries.shape[0] // QB
    return pl.pallas_call(
        attend_kernel,
        out_shape=jax.ShapeDtypeStruct(queries.shape, queries.dtype),
        grid_spec=pltpu.PrefetchScalarGridSpec(
            num_scalar_prefetch=1,
            grid=(query_blocks,),
            in_specs=[
                pl.BlockSpec((QB, H * DH), lambda i, pos: (i, 0)),
                pl.BlockSpec(memory_space=pl.ANY),
            ],
            out_specs=pl.BlockSpec((QB, H * DH), lambda i, pos: (i, 0)),
            scratch_shapes=[
                pltpu.VMEM((2, TOPN, BLOCK, 2 * DH), tile_table.dtype),
                pltpu.SemaphoreType.DMA((2, TOPN)),
            ],
        ),
        compiler_params=pltpu.CompilerParams(dimension_semantics=("arbitrary",)),
        cost_estimate=pl.CostEstimate(
            flops=4 * queries.shape[0] * H * TOPN * BLOCK * DH,
            transcendentals=queries.shape[0] * H * TOPN * BLOCK,
            bytes_accessed=2 * queries.size * 2 + query_blocks * TOPN * BLOCK * 2 * DH * 2,
        ),
    )(positions, queries, tile_table)


def solution(mesh):
    placed = (
        P(("pb", "kv"), None),
        P(("kv", "pb"), None),
        P(("kv", "pb"), None),
        P(("pb", "kv"), None),
    )
    return jax.shard_map(
        per_device, mesh=mesh, in_specs=placed, out_specs=P(("pb", "kv"), None), check_vma=False
    )
```

```python
import math

import jax
import jax.numpy as jnp
from jax import lax
from jax.experimental import pallas as pl
from jax.experimental.pallas import tpu as pltpu
from jax.sharding import PartitionSpec as P

H = 8
DH = 128
BLOCK = 64
TOPN = 16
QB = 64
CAP = 2


def holdings(wanted, owner, blocks_here):
    local_ids = owner * blocks_here + jnp.arange(blocks_here, dtype=jnp.int32)
    hits = (wanted[:, None] == local_ids[None, :]).astype(jnp.int32)
    present = jnp.max(hits, axis=0)
    return (present, jnp.cumsum(present) - present)


def slot_lists(present, slot_rank, slots):
    local_ids = jnp.arange(present.shape[-1], dtype=jnp.int32)
    slot_ids = jnp.arange(slots, dtype=jnp.int32)
    matches = (present[..., :, None] == 1) & (slot_rank[..., :, None] == slot_ids)
    return jnp.sum(jnp.where(matches, local_ids[:, None], 0), axis=-2)


def per_device(queries, keys, values, selected):
    pb_count = lax.axis_size("pb")
    kv_count = lax.axis_size("kv")
    devices = pb_count * kv_count
    blocks_here = keys.shape[0] // BLOCK
    query_blocks = queries.shape[0] // QB
    column_blocks = pb_count * blocks_here
    tiles_local = jnp.concatenate(
        [keys.reshape(blocks_here, BLOCK, DH), values.reshape(blocks_here, BLOCK, DH)], axis=2
    )
    column = lax.all_gather(tiles_local, "pb", axis=0, tiled=True)
    slots = CAP
    wanted = selected.reshape(-1)
    owners = jnp.arange(devices, dtype=jnp.int32)
    present, slot_rank = jax.vmap(lambda owner: holdings(wanted, owner, blocks_here))(owners)
    owner_lists = slot_lists(present, slot_rank, slots)
    by_column = owner_lists.reshape(kv_count, pb_count, slots) + (
        jnp.arange(pb_count, dtype=jnp.int32)[None, :, None] * blocks_here
    )
    by_column = by_column.reshape(kv_count, pb_count * slots)
    asked_for = lax.all_to_all(by_column, "kv", split_axis=0, concat_axis=0, tiled=True)
    me_kv = lax.axis_index("kv")
    end_pick = jnp.where(me_kv == kv_count - 1, column_blocks - 1, 0).astype(jnp.int32)
    picks = jnp.concatenate(
        [asked_for.reshape(kv_count, pb_count * slots), jnp.broadcast_to(end_pick, (kv_count, 1))], axis=1
    )
    outgoing = jnp.take(column, picks.reshape(-1), axis=0, mode="clip").reshape(
        kv_count, pb_count * slots + 1, BLOCK, 2 * DH
    )
    fetched = exchange(outgoing)
    tile_table = fetched.reshape(devices * slots + kv_count, BLOCK, 2 * DH)
    owner_of = selected // blocks_here
    positions = owner_of * slots + jnp.take(slot_rank.reshape(-1), selected)
    positions = positions + owner_of // pb_count
    row = pb_count * slots + 1
    leading_positions = jnp.broadcast_to(
        jnp.array([row - 1, kv_count * row - 1], jnp.int32), (query_blocks, 2)
    )
    positions = jnp.concatenate([leading_positions, positions], axis=1)
    positions = jnp.clip(positions, 0, tile_table.shape[0] - 1).reshape(-1)
    return attend_blocks(queries, tile_table, positions)


HEAD_GROUP = 4


SIDE = 4
STEPS = [(dx, dy) for dy in range(SIDE) for dx in range(SIDE) if (dx, dy) != (0, 0)]
DIRECT = [(dx, dy) for (dx, dy) in STEPS if dx != SIDE // 2 and dy != SIDE // 2]
FAR = [(dx, dy) for (dx, dy) in STEPS if dx == SIDE // 2 or dy == SIDE // 2]


RELAY_DIR = -1
RELAY_ROWS = 13


def relay_of(dx, dy):
    return (RELAY_DIR if dx == SIDE // 2 else 0, RELAY_DIR if dy == SIDE // 2 else 0)


def exchange_kernel(out_hbm, fetched_hbm, relay_hbm, d_send, d_recv, r_send, r_recv, f_send, f_recv, local_sem):
    rows = out_hbm.shape[1]
    cut = RELAY_ROWS
    me = lax.axis_index("kv")
    line = lax.axis_index("pb")
    mx = me % SIDE
    my = me // SIDE

    def at(dx, dy):
        return ((my + dy + SIDE) % SIDE) * SIDE + (mx + dx + SIDE) % SIDE

    def remote(src, dst, send, recv, target):
        return pltpu.make_async_remote_copy(
            src_ref=src, dst_ref=dst, send_sem=send, recv_sem=recv,
            device_id=(line, target), device_id_type=pl.DeviceIdType.MESH,
        )

    barrier = pltpu.get_barrier_semaphore()
    for dx, dy in STEPS:
        pl.semaphore_signal(
            barrier, inc=1, device_id=(line, at(dx, dy)), device_id_type=pl.DeviceIdType.MESH
        )
    pl.semaphore_wait(barrier, len(STEPS))
    local = pltpu.make_async_copy(out_hbm.at[me], fetched_hbm.at[me], local_sem)
    local.start()
    sent = []
    for t, (dx, dy) in enumerate(FAR):
        rx, ry = relay_of(dx, dy)
        copy = remote(
            out_hbm.at[at(dx, dy), pl.ds(0, cut)], relay_hbm.at[t],
            r_send.at[t], r_recv.at[t], at(rx, ry),
        )
        copy.start()
        sent.append(copy)
    for dx, dy in STEPS:
        k = dy * SIDE + dx
        lo = cut if (dx, dy) in FAR else 0
        copy = remote(
            out_hbm.at[at(dx, dy), pl.ds(lo, rows - lo)], fetched_hbm.at[me, pl.ds(lo, rows - lo)],
            d_send.at[k], d_recv.at[k], at(dx, dy),
        )
        copy.start()
        sent.append(copy)
    for t, (dx, dy) in enumerate(FAR):
        rx, ry = relay_of(dx, dy)
        held = relay_hbm.at[t]
        remote(held, held, r_send.at[t], r_recv.at[t], at(-rx, -ry)).wait_recv()
        copy = remote(
            held, fetched_hbm.at[at(-rx, -ry), pl.ds(0, cut)],
            f_send.at[t], f_recv.at[t], at(dx - rx, dy - ry),
        )
        copy.start()
        sent.append(copy)
    for copy in sent:
        copy.wait_send()
    for dx, dy in STEPS:
        k = dy * SIDE + dx
        lo = cut if (dx, dy) in FAR else 0
        source = at(-dx, -dy)
        part = fetched_hbm.at[source, pl.ds(lo, rows - lo)]
        remote(part, part, d_send.at[k], d_recv.at[k], source).wait_recv()
    for t, (dx, dy) in enumerate(FAR):
        source = at(-dx, -dy)
        part = fetched_hbm.at[source, pl.ds(0, cut)]
        remote(part, part, f_send.at[t], f_recv.at[t], source).wait_recv()
    local.wait()


def exchange(outgoing):
    n, rows = outgoing.shape[:2]
    flows = len(FAR)
    fetched, _ = pl.pallas_call(
        exchange_kernel,
        out_shape=(
            jax.ShapeDtypeStruct(outgoing.shape, outgoing.dtype),
            jax.ShapeDtypeStruct((flows, RELAY_ROWS) + outgoing.shape[2:], outgoing.dtype),
        ),
        in_specs=[pl.BlockSpec(memory_space=pl.ANY)],
        out_specs=(pl.BlockSpec(memory_space=pl.ANY), pl.BlockSpec(memory_space=pl.ANY)),
        scratch_shapes=[
            pltpu.SemaphoreType.DMA((n,)),
            pltpu.SemaphoreType.DMA((n,)),
            pltpu.SemaphoreType.DMA((flows,)),
            pltpu.SemaphoreType.DMA((flows,)),
            pltpu.SemaphoreType.DMA((flows,)),
            pltpu.SemaphoreType.DMA((flows,)),
            pltpu.SemaphoreType.DMA(()),
        ],
        compiler_params=pltpu.CompilerParams(collective_id=0, has_side_effects=True),
    )(outgoing)
    return fetched


def attend_kernel(pos_ref, q_ref, table_hbm, o_ref, kvbuf, sems):
    step = pl.program_id(0)
    steps = pl.num_programs(0)

    def fetch(block, slot):
        for j in range(TOPN):
            pltpu.make_async_copy(
                table_hbm.at[pos_ref[block * TOPN + j]], kvbuf.at[slot, j], sems.at[slot, j]
            ).start()

    @pl.when(step == 0)
    def _():
        fetch(0, 0)

    slot = step % 2

    @pl.when(step + 1 < steps)
    def _():
        fetch(step + 1, 1 - slot)

    for j in range(TOPN):
        pltpu.make_async_copy(table_hbm.at[0], kvbuf.at[slot, j], sems.at[slot, j]).wait()
    tiles = kvbuf[slot]
    k_rows = tiles[:, :, :DH].reshape(TOPN * BLOCK, DH)
    v_rows = tiles[:, :, DH:].reshape(TOPN * BLOCK, DH)
    for g in range(H // HEAD_GROUP):
        heads = range(g * HEAD_GROUP, (g + 1) * HEAD_GROUP)
        q_rows = jnp.concatenate([q_ref[:, h * DH : (h + 1) * DH] for h in heads], axis=0)
        scores = lax.dot_general(
            q_rows, k_rows, (((1,), (1,)), ((), ())), preferred_element_type=jnp.float32
        ) * DH ** (-0.5)
        weights = jnp.exp(scores - jnp.max(scores, axis=-1, keepdims=True))
        totals = jnp.sum(weights, axis=-1, keepdims=True)
        weighted = jnp.dot(
            weights.astype(jnp.bfloat16), v_rows, preferred_element_type=jnp.float32
        )
        out = (weighted / totals).astype(o_ref.dtype)
        for i, h in enumerate(heads):
            o_ref[:, h * DH : (h + 1) * DH] = out[i * QB : (i + 1) * QB]


def attend_blocks(queries, tile_table, positions):
    query_blocks = queries.shape[0] // QB
    return pl.pallas_call(
        attend_kernel,
        out_shape=jax.ShapeDtypeStruct(queries.shape, queries.dtype),
        grid_spec=pltpu.PrefetchScalarGridSpec(
            num_scalar_prefetch=1,
            grid=(query_blocks,),
            in_specs=[
                pl.BlockSpec((QB, H * DH), lambda i, pos: (i, 0)),
                pl.BlockSpec(memory_space=pl.ANY),
            ],
            out_specs=pl.BlockSpec((QB, H * DH), lambda i, pos: (i, 0)),
            scratch_shapes=[
                pltpu.VMEM((2, TOPN, BLOCK, 2 * DH), tile_table.dtype),
                pltpu.SemaphoreType.DMA((2, TOPN)),
            ],
        ),
        compiler_params=pltpu.CompilerParams(dimension_semantics=("arbitrary",)),
        cost_estimate=pl.CostEstimate(
            flops=4 * queries.shape[0] * H * TOPN * BLOCK * DH,
            transcendentals=queries.shape[0] * H * TOPN * BLOCK,
            bytes_accessed=2 * queries.size * 2 + query_blocks * TOPN * BLOCK * 2 * DH * 2,
        ),
    )(positions, queries, tile_table)


def solution(mesh):
    placed = (
        P(("pb", "kv"), None),
        P(("kv", "pb"), None),
        P(("kv", "pb"), None),
        P(("pb", "kv"), None),
    )
    return jax.shard_map(
        per_device, mesh=mesh, in_specs=placed, out_specs=P(("pb", "kv"), None), check_vma=False
    )
```

```python
import math

import jax
import jax.numpy as jnp
from jax import lax
from jax.experimental import pallas as pl
from jax.experimental.pallas import tpu as pltpu
from jax.sharding import PartitionSpec as P

H = 8
DH = 128
BLOCK = 64
TOPN = 16
QB = 64
CAP = 2


def holdings(wanted, owner, blocks_here):
    local_ids = owner * blocks_here + jnp.arange(blocks_here, dtype=jnp.int32)
    hits = (wanted[:, None] == local_ids[None, :]).astype(jnp.int32)
    present = jnp.max(hits, axis=0)
    return (present, jnp.cumsum(present) - present)


def slot_lists(present, slot_rank, slots):
    local_ids = jnp.arange(present.shape[-1], dtype=jnp.int32)
    slot_ids = jnp.arange(slots, dtype=jnp.int32)
    matches = (present[..., :, None] == 1) & (slot_rank[..., :, None] == slot_ids)
    return jnp.sum(jnp.where(matches, local_ids[:, None], 0), axis=-2)


def per_device(queries, keys, values, selected):
    pb_count = lax.axis_size("pb")
    kv_count = lax.axis_size("kv")
    devices = pb_count * kv_count
    blocks_here = keys.shape[0] // BLOCK
    query_blocks = queries.shape[0] // QB
    column_blocks = pb_count * blocks_here
    tiles_local = jnp.concatenate(
        [keys.reshape(blocks_here, BLOCK, DH), values.reshape(blocks_here, BLOCK, DH)], axis=2
    )
    column = lax.all_gather(tiles_local, "pb", axis=0, tiled=True)
    slots = CAP
    wanted = selected.reshape(-1)
    owners = jnp.arange(devices, dtype=jnp.int32)
    present, slot_rank = jax.vmap(lambda owner: holdings(wanted, owner, blocks_here))(owners)
    owner_lists = slot_lists(present, slot_rank, slots)
    by_column = owner_lists.reshape(kv_count, pb_count, slots) + (
        jnp.arange(pb_count, dtype=jnp.int32)[None, :, None] * blocks_here
    )
    by_column = by_column.reshape(kv_count, pb_count * slots)
    asked_for = lax.all_to_all(by_column, "kv", split_axis=0, concat_axis=0, tiled=True)
    me_kv = lax.axis_index("kv")
    end_pick = jnp.where(me_kv == kv_count - 1, column_blocks - 1, 0).astype(jnp.int32)
    picks = jnp.concatenate(
        [asked_for.reshape(kv_count, pb_count * slots), jnp.broadcast_to(end_pick, (kv_count, 1))], axis=1
    )
    outgoing = jnp.take(column, picks.reshape(-1), axis=0, mode="clip").reshape(
        kv_count, pb_count * slots + 1, BLOCK, 2 * DH
    )
    fetched = exchange(outgoing)
    tile_table = fetched.reshape(devices * slots + kv_count, BLOCK, 2 * DH)
    owner_of = selected // blocks_here
    positions = owner_of * slots + jnp.take(slot_rank.reshape(-1), selected)
    positions = positions + owner_of // pb_count
    row = pb_count * slots + 1
    leading_positions = jnp.broadcast_to(
        jnp.array([row - 1, kv_count * row - 1], jnp.int32), (query_blocks, 2)
    )
    positions = jnp.concatenate([leading_positions, positions], axis=1)
    positions = jnp.clip(positions, 0, tile_table.shape[0] - 1).reshape(-1)
    return attend_blocks(queries, tile_table, positions)


HEAD_GROUP = 4


SIDE = 4
STEPS = [(dx, dy) for dy in range(SIDE) for dx in range(SIDE) if (dx, dy) != (0, 0)]
DIRECT = [(dx, dy) for (dx, dy) in STEPS if dx != SIDE // 2 and dy != SIDE // 2]
FAR = [(dx, dy) for (dx, dy) in STEPS if dx == SIDE // 2 or dy == SIDE // 2]


RELAY_DIR = 1
RELAY_ROWS = 13


def relay_of(dx, dy):
    return (RELAY_DIR if dx == SIDE // 2 else 0, RELAY_DIR if dy == SIDE // 2 else 0)


def exchange_kernel(out_hbm, fetched_hbm, relay_hbm, d_send, d_recv, r_send, r_recv, f_send, f_recv, local_sem):
    rows = out_hbm.shape[1]
    cut = RELAY_ROWS
    me = lax.axis_index("kv")
    line = lax.axis_index("pb")
    mx = me % SIDE
    my = me // SIDE

    def at(dx, dy):
        return ((my + dy + SIDE) % SIDE) * SIDE + (mx + dx + SIDE) % SIDE

    def remote(src, dst, send, recv, target):
        return pltpu.make_async_remote_copy(
            src_ref=src, dst_ref=dst, send_sem=send, recv_sem=recv,
            device_id=(line, target), device_id_type=pl.DeviceIdType.MESH,
        )

    barrier = pltpu.get_barrier_semaphore()
    for dx, dy in STEPS:
        pl.semaphore_signal(
            barrier, inc=1, device_id=(line, at(dx, dy)), device_id_type=pl.DeviceIdType.MESH
        )
    pl.semaphore_wait(barrier, len(STEPS))
    local = pltpu.make_async_copy(out_hbm.at[me], fetched_hbm.at[me], local_sem)
    local.start()
    sent = []
    for t, (dx, dy) in enumerate(FAR):
        rx, ry = relay_of(dx, dy)
        copy = remote(
            out_hbm.at[at(dx, dy), pl.ds(0, cut)], relay_hbm.at[t],
            r_send.at[t], r_recv.at[t], at(rx, ry),
        )
        copy.start()
        sent.append(copy)
    for dx, dy in STEPS:
        k = dy * SIDE + dx
        lo = cut if (dx, dy) in FAR else 0
        copy = remote(
            out_hbm.at[at(dx, dy), pl.ds(lo, rows - lo)], fetched_hbm.at[me, pl.ds(lo, rows - lo)],
            d_send.at[k], d_recv.at[k], at(dx, dy),
        )
        copy.start()
        sent.append(copy)
    for t, (dx, dy) in enumerate(FAR):
        rx, ry = relay_of(dx, dy)
        held = relay_hbm.at[t]
        remote(held, held, r_send.at[t], r_recv.at[t], at(-rx, -ry)).wait_recv()
        copy = remote(
            held, fetched_hbm.at[at(-rx, -ry), pl.ds(0, cut)],
            f_send.at[t], f_recv.at[t], at(dx - rx, dy - ry),
        )
        copy.start()
        sent.append(copy)
    for copy in sent:
        copy.wait_send()
    for dx, dy in STEPS:
        k = dy * SIDE + dx
        lo = cut if (dx, dy) in FAR else 0
        source = at(-dx, -dy)
        part = fetched_hbm.at[source, pl.ds(lo, rows - lo)]
        remote(part, part, d_send.at[k], d_recv.at[k], source).wait_recv()
    for t, (dx, dy) in enumerate(FAR):
        source = at(-dx, -dy)
        part = fetched_hbm.at[source, pl.ds(0, cut)]
        remote(part, part, f_send.at[t], f_recv.at[t], source).wait_recv()
    local.wait()


def exchange(outgoing):
    n, rows = outgoing.shape[:2]
    flows = len(FAR)
    fetched, _ = pl.pallas_call(
        exchange_kernel,
        out_shape=(
            jax.ShapeDtypeStruct(outgoing.shape, outgoing.dtype),
            jax.ShapeDtypeStruct((flows, RELAY_ROWS) + outgoing.shape[2:], outgoing.dtype),
        ),
        in_specs=[pl.BlockSpec(memory_space=pl.ANY)],
        out_specs=(pl.BlockSpec(memory_space=pl.ANY), pl.BlockSpec(memory_space=pl.ANY)),
        scratch_shapes=[
            pltpu.SemaphoreType.DMA((n,)),
            pltpu.SemaphoreType.DMA((n,)),
            pltpu.SemaphoreType.DMA((flows,)),
            pltpu.SemaphoreType.DMA((flows,)),
            pltpu.SemaphoreType.DMA((flows,)),
            pltpu.SemaphoreType.DMA((flows,)),
            pltpu.SemaphoreType.DMA(()),
        ],
        compiler_params=pltpu.CompilerParams(collective_id=0, has_side_effects=True),
    )(outgoing)
    return fetched


def attend_kernel(pos_ref, q_ref, table_hbm, o_ref, kvbuf, sems):
    step = pl.program_id(0)
    steps = pl.num_programs(0)

    def fetch(block, slot):
        for j in range(TOPN):
            pltpu.make_async_copy(
                table_hbm.at[pos_ref[block * TOPN + j]], kvbuf.at[slot, j], sems.at[slot, j]
            ).start()

    @pl.when(step == 0)
    def _():
        fetch(0, 0)

    slot = step % 2

    @pl.when(step + 1 < steps)
    def _():
        fetch(step + 1, 1 - slot)

    for j in range(TOPN):
        pltpu.make_async_copy(table_hbm.at[0], kvbuf.at[slot, j], sems.at[slot, j]).wait()
    tiles = kvbuf[slot]
    k_rows = tiles[:, :, :DH].reshape(TOPN * BLOCK, DH)
    v_rows = tiles[:, :, DH:].reshape(TOPN * BLOCK, DH)
    for g in range(H // HEAD_GROUP):
        heads = range(g * HEAD_GROUP, (g + 1) * HEAD_GROUP)
        q_rows = jnp.concatenate([q_ref[:, h * DH : (h + 1) * DH] for h in heads], axis=0)
        scores = lax.dot_general(
            q_rows, k_rows, (((1,), (1,)), ((), ())), preferred_element_type=jnp.float32
        ) * DH ** (-0.5)
        weights = jnp.exp(scores - jnp.max(scores, axis=-1, keepdims=True))
        totals = jnp.sum(weights, axis=-1, keepdims=True)
        weighted = jnp.dot(
            weights.astype(jnp.bfloat16), v_rows, preferred_element_type=jnp.float32
        )
        out = (weighted / totals).astype(o_ref.dtype)
        for i, h in enumerate(heads):
            o_ref[:, h * DH : (h + 1) * DH] = out[i * QB : (i + 1) * QB]


def attend_blocks(queries, tile_table, positions):
    query_blocks = queries.shape[0] // QB
    return pl.pallas_call(
        attend_kernel,
        out_shape=jax.ShapeDtypeStruct(queries.shape, queries.dtype),
        grid_spec=pltpu.PrefetchScalarGridSpec(
            num_scalar_prefetch=1,
            grid=(query_blocks,),
            in_specs=[
                pl.BlockSpec((QB, H * DH), lambda i, pos: (i, 0)),
                pl.BlockSpec(memory_space=pl.ANY),
            ],
            out_specs=pl.BlockSpec((QB, H * DH), lambda i, pos: (i, 0)),
            scratch_shapes=[
                pltpu.VMEM((2, TOPN, BLOCK, 2 * DH), tile_table.dtype),
                pltpu.SemaphoreType.DMA((2, TOPN)),
            ],
        ),
        compiler_params=pltpu.CompilerParams(dimension_semantics=("arbitrary",)),
        cost_estimate=pl.CostEstimate(
            flops=4 * queries.shape[0] * H * TOPN * BLOCK * DH,
            transcendentals=queries.shape[0] * H * TOPN * BLOCK,
            bytes_accessed=2 * queries.size * 2 + query_blocks * TOPN * BLOCK * 2 * DH * 2,
        ),
    )(positions, queries, tile_table)


def solution(mesh):
    placed = (
        P(("pb", "kv"), None),
        P(("kv", "pb"), None),
        P(("kv", "pb"), None),
        P(("pb", "kv"), None),
    )
    return jax.shard_map(
        per_device, mesh=mesh, in_specs=placed, out_specs=P(("pb", "kv"), None), check_vma=False
    )
```

```python
import math

import jax
import jax.numpy as jnp
from jax import lax
from jax.experimental import pallas as pl
from jax.experimental.pallas import tpu as pltpu
from jax.sharding import PartitionSpec as P

H = 8
DH = 128
BLOCK = 64
TOPN = 16
QB = 64
CAP = 2


def holdings(wanted, owner, blocks_here):
    local_ids = owner * blocks_here + jnp.arange(blocks_here, dtype=jnp.int32)
    hits = (wanted[:, None] == local_ids[None, :]).astype(jnp.int32)
    present = jnp.max(hits, axis=0)
    return (present, jnp.cumsum(present) - present)


def slot_lists(present, slot_rank, slots):
    local_ids = jnp.arange(present.shape[-1], dtype=jnp.int32)
    slot_ids = jnp.arange(slots, dtype=jnp.int32)
    matches = (present[..., :, None] == 1) & (slot_rank[..., :, None] == slot_ids)
    return jnp.sum(jnp.where(matches, local_ids[:, None], 0), axis=-2)


def per_device(queries, keys, values, selected):
    pb_count = lax.axis_size("pb")
    kv_count = lax.axis_size("kv")
    devices = pb_count * kv_count
    blocks_here = keys.shape[0] // BLOCK
    query_blocks = queries.shape[0] // QB
    column_blocks = pb_count * blocks_here
    tiles_local = jnp.concatenate(
        [keys.reshape(blocks_here, BLOCK, DH), values.reshape(blocks_here, BLOCK, DH)], axis=2
    )
    column = lax.all_gather(tiles_local, "pb", axis=0, tiled=True)
    slots = CAP
    wanted = selected.reshape(-1)
    owners = jnp.arange(devices, dtype=jnp.int32)
    present, slot_rank = jax.vmap(lambda owner: holdings(wanted, owner, blocks_here))(owners)
    owner_lists = slot_lists(present, slot_rank, slots)
    by_column = owner_lists.reshape(kv_count, pb_count, slots) + (
        jnp.arange(pb_count, dtype=jnp.int32)[None, :, None] * blocks_here
    )
    by_column = by_column.reshape(kv_count, pb_count * slots)
    asked_for = lax.all_to_all(by_column, "kv", split_axis=0, concat_axis=0, tiled=True)
    me_kv = lax.axis_index("kv")
    end_pick = jnp.where(me_kv == kv_count - 1, column_blocks - 1, 0).astype(jnp.int32)
    picks = jnp.concatenate(
        [asked_for.reshape(kv_count, pb_count * slots), jnp.broadcast_to(end_pick, (kv_count, 1))], axis=1
    )
    outgoing = jnp.take(column, picks.reshape(-1), axis=0, mode="clip").reshape(
        kv_count, pb_count * slots + 1, BLOCK, 2 * DH
    )
    fetched = exchange(outgoing)
    tile_table = fetched.reshape(devices * slots + kv_count, BLOCK, 2 * DH)
    owner_of = selected // blocks_here
    positions = owner_of * slots + jnp.take(slot_rank.reshape(-1), selected)
    positions = positions + owner_of // pb_count
    row = pb_count * slots + 1
    leading_positions = jnp.broadcast_to(
        jnp.array([row - 1, kv_count * row - 1], jnp.int32), (query_blocks, 2)
    )
    positions = jnp.concatenate([leading_positions, positions], axis=1)
    positions = jnp.clip(positions, 0, tile_table.shape[0] - 1).reshape(-1)
    return attend_blocks(queries, tile_table, positions)


HEAD_GROUP = 8


SIDE = 4
STEPS = [(dx, dy) for dy in range(SIDE) for dx in range(SIDE) if (dx, dy) != (0, 0)]
DIRECT = [(dx, dy) for (dx, dy) in STEPS if dx != SIDE // 2 and dy != SIDE // 2]
FAR = [(dx, dy) for (dx, dy) in STEPS if dx == SIDE // 2 or dy == SIDE // 2]


def relays_of(dx, dy):
    if dx == SIDE // 2 and dy == SIDE // 2:
        return [(-1, -1), (1, 1)]
    if dx == SIDE // 2:
        return [(-1, 0), (1, 0)]
    return [(0, -1), (0, 1)]


def exchange_kernel(out_hbm, fetched_hbm, relay_hbm, d_send, d_recv, r_send, r_recv, f_send, f_recv, local_sem):
    rows = out_hbm.shape[1]
    parts = [(0, rows // 2), (rows // 2, rows - rows // 2)]
    me = lax.axis_index("kv")
    line = lax.axis_index("pb")
    mx = me % SIDE
    my = me // SIDE

    def at(dx, dy):
        return ((my + dy + SIDE) % SIDE) * SIDE + (mx + dx + SIDE) % SIDE

    def remote(src, dst, send, recv, target):
        return pltpu.make_async_remote_copy(
            src_ref=src, dst_ref=dst, send_sem=send, recv_sem=recv,
            device_id=(line, target), device_id_type=pl.DeviceIdType.MESH,
        )

    barrier = pltpu.get_barrier_semaphore()
    for dx, dy in STEPS:
        pl.semaphore_signal(
            barrier, inc=1, device_id=(line, at(dx, dy)), device_id_type=pl.DeviceIdType.MESH
        )
    pl.semaphore_wait(barrier, len(STEPS))
    local = pltpu.make_async_copy(out_hbm.at[me], fetched_hbm.at[me], local_sem)
    local.start()
    sent = []
    for t, (dx, dy) in enumerate(FAR):
        for h, (rx, ry) in enumerate(relays_of(dx, dy)):
            f = 2 * t + h
            lo, size = parts[h]
            copy = remote(
                out_hbm.at[at(dx, dy), pl.ds(lo, size)], relay_hbm.at[f, pl.ds(0, size)],
                r_send.at[f], r_recv.at[f], at(rx, ry),
            )
            copy.start()
            sent.append(copy)
    for dx, dy in DIRECT:
        k = dy * SIDE + dx
        copy = remote(out_hbm.at[at(dx, dy)], fetched_hbm.at[me], d_send.at[k], d_recv.at[k], at(dx, dy))
        copy.start()
        sent.append(copy)
    for t, (dx, dy) in enumerate(FAR):
        for h, (rx, ry) in enumerate(relays_of(dx, dy)):
            f = 2 * t + h
            lo, size = parts[h]
            held = relay_hbm.at[f, pl.ds(0, size)]
            remote(held, held, r_send.at[f], r_recv.at[f], at(-rx, -ry)).wait_recv()
            copy = remote(
                held, fetched_hbm.at[at(-rx, -ry), pl.ds(lo, size)],
                f_send.at[f], f_recv.at[f], at(dx - rx, dy - ry),
            )
            copy.start()
            sent.append(copy)
    for copy in sent:
        copy.wait_send()
    for dx, dy in DIRECT:
        k = dy * SIDE + dx
        source = at(-dx, -dy)
        remote(
            out_hbm.at[source], fetched_hbm.at[source], d_send.at[k], d_recv.at[k], source
        ).wait_recv()
    for t, (dx, dy) in enumerate(FAR):
        for h in range(2):
            f = 2 * t + h
            lo, size = parts[h]
            source = at(-dx, -dy)
            part = fetched_hbm.at[source, pl.ds(lo, size)]
            remote(part, part, f_send.at[f], f_recv.at[f], source).wait_recv()
    local.wait()


def exchange(outgoing):
    n, rows = outgoing.shape[:2]
    flows = 2 * len(FAR)
    fetched, _ = pl.pallas_call(
        exchange_kernel,
        out_shape=(
            jax.ShapeDtypeStruct(outgoing.shape, outgoing.dtype),
            jax.ShapeDtypeStruct((flows, rows - rows // 2) + outgoing.shape[2:], outgoing.dtype),
        ),
        in_specs=[pl.BlockSpec(memory_space=pl.ANY)],
        out_specs=(pl.BlockSpec(memory_space=pl.ANY), pl.BlockSpec(memory_space=pl.ANY)),
        scratch_shapes=[
            pltpu.SemaphoreType.DMA((n,)),
            pltpu.SemaphoreType.DMA((n,)),
            pltpu.SemaphoreType.DMA((flows,)),
            pltpu.SemaphoreType.DMA((flows,)),
            pltpu.SemaphoreType.DMA((flows,)),
            pltpu.SemaphoreType.DMA((flows,)),
            pltpu.SemaphoreType.DMA(()),
        ],
        compiler_params=pltpu.CompilerParams(collective_id=0, has_side_effects=True),
    )(outgoing)
    return fetched


def attend_kernel(pos_ref, q_ref, table_hbm, o_ref, kvbuf, sems):
    step = pl.program_id(0)
    steps = pl.num_programs(0)

    def fetch(block, slot):
        for j in range(TOPN):
            pltpu.make_async_copy(
                table_hbm.at[pos_ref[block * TOPN + j]], kvbuf.at[slot, j], sems.at[slot, j]
            ).start()

    @pl.when(step == 0)
    def _():
        fetch(0, 0)

    slot = step % 2

    @pl.when(step + 1 < steps)
    def _():
        fetch(step + 1, 1 - slot)

    for j in range(TOPN):
        pltpu.make_async_copy(table_hbm.at[0], kvbuf.at[slot, j], sems.at[slot, j]).wait()
    tiles = kvbuf[slot]
    k_rows = tiles[:, :, :DH].reshape(TOPN * BLOCK, DH)
    v_rows = tiles[:, :, DH:].reshape(TOPN * BLOCK, DH)
    for g in range(H // HEAD_GROUP):
        heads = range(g * HEAD_GROUP, (g + 1) * HEAD_GROUP)
        q_rows = jnp.concatenate([q_ref[:, h * DH : (h + 1) * DH] for h in heads], axis=0)
        scores = lax.dot_general(
            q_rows, k_rows, (((1,), (1,)), ((), ())), preferred_element_type=jnp.float32
        ) * DH ** (-0.5)
        weights = jnp.exp(scores - jnp.max(scores, axis=-1, keepdims=True))
        totals = jnp.sum(weights, axis=-1, keepdims=True)
        weighted = jnp.dot(
            weights.astype(jnp.bfloat16), v_rows, preferred_element_type=jnp.float32
        )
        out = (weighted / totals).astype(o_ref.dtype)
        for i, h in enumerate(heads):
            o_ref[:, h * DH : (h + 1) * DH] = out[i * QB : (i + 1) * QB]


def attend_blocks(queries, tile_table, positions):
    query_blocks = queries.shape[0] // QB
    return pl.pallas_call(
        attend_kernel,
        out_shape=jax.ShapeDtypeStruct(queries.shape, queries.dtype),
        grid_spec=pltpu.PrefetchScalarGridSpec(
            num_scalar_prefetch=1,
            grid=(query_blocks,),
            in_specs=[
                pl.BlockSpec((QB, H * DH), lambda i, pos: (i, 0)),
                pl.BlockSpec(memory_space=pl.ANY),
            ],
            out_specs=pl.BlockSpec((QB, H * DH), lambda i, pos: (i, 0)),
            scratch_shapes=[
                pltpu.VMEM((2, TOPN, BLOCK, 2 * DH), tile_table.dtype),
                pltpu.SemaphoreType.DMA((2, TOPN)),
            ],
        ),
        compiler_params=pltpu.CompilerParams(dimension_semantics=("arbitrary",)),
        cost_estimate=pl.CostEstimate(
            flops=4 * queries.shape[0] * H * TOPN * BLOCK * DH,
            transcendentals=queries.shape[0] * H * TOPN * BLOCK,
            bytes_accessed=2 * queries.size * 2 + query_blocks * TOPN * BLOCK * 2 * DH * 2,
        ),
    )(positions, queries, tile_table)


def solution(mesh):
    placed = (
        P(("pb", "kv"), None),
        P(("kv", "pb"), None),
        P(("kv", "pb"), None),
        P(("pb", "kv"), None),
    )
    return jax.shard_map(
        per_device, mesh=mesh, in_specs=placed, out_specs=P(("pb", "kv"), None), check_vma=False
    )
```

```python
import math

import jax
import jax.numpy as jnp
from jax import lax
from jax.experimental import pallas as pl
from jax.experimental.pallas import tpu as pltpu
from jax.sharding import PartitionSpec as P

H = 8
DH = 128
BLOCK = 64
TOPN = 16
QB = 64
CAP = 2


def holdings(wanted, owner, blocks_here):
    local_ids = owner * blocks_here + jnp.arange(blocks_here, dtype=jnp.int32)
    hits = (wanted[:, None] == local_ids[None, :]).astype(jnp.int32)
    present = jnp.max(hits, axis=0)
    return (present, jnp.cumsum(present) - present)


def slot_lists(present, slot_rank, slots):
    local_ids = jnp.arange(present.shape[-1], dtype=jnp.int32)
    slot_ids = jnp.arange(slots, dtype=jnp.int32)
    matches = (present[..., :, None] == 1) & (slot_rank[..., :, None] == slot_ids)
    return jnp.sum(jnp.where(matches, local_ids[:, None], 0), axis=-2)


def per_device(queries, keys, values, selected):
    pb_count = lax.axis_size("pb")
    kv_count = lax.axis_size("kv")
    devices = pb_count * kv_count
    blocks_here = keys.shape[0] // BLOCK
    query_blocks = queries.shape[0] // QB
    column_blocks = pb_count * blocks_here
    tiles_local = jnp.concatenate(
        [keys.reshape(blocks_here, BLOCK, DH), values.reshape(blocks_here, BLOCK, DH)], axis=2
    )
    column = lax.all_gather(tiles_local, "pb", axis=0, tiled=True)
    slots = CAP
    wanted = selected.reshape(-1)
    owners = jnp.arange(devices, dtype=jnp.int32)
    present, slot_rank = jax.vmap(lambda owner: holdings(wanted, owner, blocks_here))(owners)
    owner_lists = slot_lists(present, slot_rank, slots)
    by_column = owner_lists.reshape(kv_count, pb_count, slots) + (
        jnp.arange(pb_count, dtype=jnp.int32)[None, :, None] * blocks_here
    )
    by_column = by_column.reshape(kv_count, pb_count * slots)
    asked_for = lax.all_to_all(by_column, "kv", split_axis=0, concat_axis=0, tiled=True)
    me_kv = lax.axis_index("kv")
    end_pick = jnp.where(me_kv == kv_count - 1, column_blocks - 1, 0).astype(jnp.int32)
    picks = jnp.concatenate(
        [asked_for.reshape(kv_count, pb_count * slots), jnp.broadcast_to(end_pick, (kv_count, 1))], axis=1
    )
    outgoing = jnp.take(column, picks.reshape(-1), axis=0, mode="clip").reshape(
        kv_count, pb_count * slots + 1, BLOCK, 2 * DH
    )
    fetched = exchange(outgoing)
    tile_table = fetched.reshape(devices * slots + kv_count, BLOCK, 2 * DH)
    owner_of = selected // blocks_here
    positions = owner_of * slots + jnp.take(slot_rank.reshape(-1), selected)
    positions = positions + owner_of // pb_count
    row = pb_count * slots + 1
    leading_positions = jnp.broadcast_to(
        jnp.array([row - 1, kv_count * row - 1], jnp.int32), (query_blocks, 2)
    )
    positions = jnp.concatenate([leading_positions, positions], axis=1)
    positions = jnp.clip(positions, 0, tile_table.shape[0] - 1).reshape(-1)
    return attend_blocks(queries, tile_table, positions)


HEAD_GROUP = 2


SIDE = 4
STEPS = [(dx, dy) for dy in range(SIDE) for dx in range(SIDE) if (dx, dy) != (0, 0)]
DIRECT = [(dx, dy) for (dx, dy) in STEPS if dx != SIDE // 2 and dy != SIDE // 2]
FAR = [(dx, dy) for (dx, dy) in STEPS if dx == SIDE // 2 or dy == SIDE // 2]


def relays_of(dx, dy):
    if dx == SIDE // 2 and dy == SIDE // 2:
        return [(-1, -1), (1, 1)]
    if dx == SIDE // 2:
        return [(-1, 0), (1, 0)]
    return [(0, -1), (0, 1)]


def exchange_kernel(out_hbm, fetched_hbm, relay_hbm, d_send, d_recv, r_send, r_recv, f_send, f_recv, local_sem):
    rows = out_hbm.shape[1]
    parts = [(0, rows // 2), (rows // 2, rows - rows // 2)]
    me = lax.axis_index("kv")
    line = lax.axis_index("pb")
    mx = me % SIDE
    my = me // SIDE

    def at(dx, dy):
        return ((my + dy + SIDE) % SIDE) * SIDE + (mx + dx + SIDE) % SIDE

    def remote(src, dst, send, recv, target):
        return pltpu.make_async_remote_copy(
            src_ref=src, dst_ref=dst, send_sem=send, recv_sem=recv,
            device_id=(line, target), device_id_type=pl.DeviceIdType.MESH,
        )

    barrier = pltpu.get_barrier_semaphore()
    for dx, dy in STEPS:
        pl.semaphore_signal(
            barrier, inc=1, device_id=(line, at(dx, dy)), device_id_type=pl.DeviceIdType.MESH
        )
    pl.semaphore_wait(barrier, len(STEPS))
    local = pltpu.make_async_copy(out_hbm.at[me], fetched_hbm.at[me], local_sem)
    local.start()
    sent = []
    for t, (dx, dy) in enumerate(FAR):
        for h, (rx, ry) in enumerate(relays_of(dx, dy)):
            f = 2 * t + h
            lo, size = parts[h]
            copy = remote(
                out_hbm.at[at(dx, dy), pl.ds(lo, size)], relay_hbm.at[f, pl.ds(0, size)],
                r_send.at[f], r_recv.at[f], at(rx, ry),
            )
            copy.start()
            sent.append(copy)
    for dx, dy in DIRECT:
        k = dy * SIDE + dx
        copy = remote(out_hbm.at[at(dx, dy)], fetched_hbm.at[me], d_send.at[k], d_recv.at[k], at(dx, dy))
        copy.start()
        sent.append(copy)
    for t, (dx, dy) in enumerate(FAR):
        for h, (rx, ry) in enumerate(relays_of(dx, dy)):
            f = 2 * t + h
            lo, size = parts[h]
            held = relay_hbm.at[f, pl.ds(0, size)]
            remote(held, held, r_send.at[f], r_recv.at[f], at(-rx, -ry)).wait_recv()
            copy = remote(
                held, fetched_hbm.at[at(-rx, -ry), pl.ds(lo, size)],
                f_send.at[f], f_recv.at[f], at(dx - rx, dy - ry),
            )
            copy.start()
            sent.append(copy)
    for copy in sent:
        copy.wait_send()
    for dx, dy in DIRECT:
        k = dy * SIDE + dx
        source = at(-dx, -dy)
        remote(
            out_hbm.at[source], fetched_hbm.at[source], d_send.at[k], d_recv.at[k], source
        ).wait_recv()
    for t, (dx, dy) in enumerate(FAR):
        for h in range(2):
            f = 2 * t + h
            lo, size = parts[h]
            source = at(-dx, -dy)
            part = fetched_hbm.at[source, pl.ds(lo, size)]
            remote(part, part, f_send.at[f], f_recv.at[f], source).wait_recv()
    local.wait()


def exchange(outgoing):
    n, rows = outgoing.shape[:2]
    flows = 2 * len(FAR)
    fetched, _ = pl.pallas_call(
        exchange_kernel,
        out_shape=(
            jax.ShapeDtypeStruct(outgoing.shape, outgoing.dtype),
            jax.ShapeDtypeStruct((flows, rows - rows // 2) + outgoing.shape[2:], outgoing.dtype),
        ),
        in_specs=[pl.BlockSpec(memory_space=pl.ANY)],
        out_specs=(pl.BlockSpec(memory_space=pl.ANY), pl.BlockSpec(memory_space=pl.ANY)),
        scratch_shapes=[
            pltpu.SemaphoreType.DMA((n,)),
            pltpu.SemaphoreType.DMA((n,)),
            pltpu.SemaphoreType.DMA((flows,)),
            pltpu.SemaphoreType.DMA((flows,)),
            pltpu.SemaphoreType.DMA((flows,)),
            pltpu.SemaphoreType.DMA((flows,)),
            pltpu.SemaphoreType.DMA(()),
        ],
        compiler_params=pltpu.CompilerParams(collective_id=0, has_side_effects=True),
    )(outgoing)
    return fetched


def attend_kernel(pos_ref, q_ref, table_hbm, o_ref, kvbuf, sems):
    step = pl.program_id(0)
    steps = pl.num_programs(0)

    def fetch(block, slot):
        for j in range(TOPN):
            pltpu.make_async_copy(
                table_hbm.at[pos_ref[block * TOPN + j]], kvbuf.at[slot, j], sems.at[slot, j]
            ).start()

    @pl.when(step == 0)
    def _():
        fetch(0, 0)

    slot = step % 2

    @pl.when(step + 1 < steps)
    def _():
        fetch(step + 1, 1 - slot)

    for j in range(TOPN):
        pltpu.make_async_copy(table_hbm.at[0], kvbuf.at[slot, j], sems.at[slot, j]).wait()
    tiles = kvbuf[slot]
    k_rows = tiles[:, :, :DH].reshape(TOPN * BLOCK, DH)
    v_rows = tiles[:, :, DH:].reshape(TOPN * BLOCK, DH)
    for g in range(H // HEAD_GROUP):
        heads = range(g * HEAD_GROUP, (g + 1) * HEAD_GROUP)
        q_rows = jnp.concatenate([q_ref[:, h * DH : (h + 1) * DH] for h in heads], axis=0)
        scores = lax.dot_general(
            q_rows, k_rows, (((1,), (1,)), ((), ())), preferred_element_type=jnp.float32
        ) * DH ** (-0.5)
        weights = jnp.exp(scores - jnp.max(scores, axis=-1, keepdims=True))
        totals = jnp.sum(weights, axis=-1, keepdims=True)
        weighted = jnp.dot(
            weights.astype(jnp.bfloat16), v_rows, preferred_element_type=jnp.float32
        )
        out = (weighted / totals).astype(o_ref.dtype)
        for i, h in enumerate(heads):
            o_ref[:, h * DH : (h + 1) * DH] = out[i * QB : (i + 1) * QB]


def attend_blocks(queries, tile_table, positions):
    query_blocks = queries.shape[0] // QB
    return pl.pallas_call(
        attend_kernel,
        out_shape=jax.ShapeDtypeStruct(queries.shape, queries.dtype),
        grid_spec=pltpu.PrefetchScalarGridSpec(
            num_scalar_prefetch=1,
            grid=(query_blocks,),
            in_specs=[
                pl.BlockSpec((QB, H * DH), lambda i, pos: (i, 0)),
                pl.BlockSpec(memory_space=pl.ANY),
            ],
            out_specs=pl.BlockSpec((QB, H * DH), lambda i, pos: (i, 0)),
            scratch_shapes=[
                pltpu.VMEM((2, TOPN, BLOCK, 2 * DH), tile_table.dtype),
                pltpu.SemaphoreType.DMA((2, TOPN)),
            ],
        ),
        compiler_params=pltpu.CompilerParams(dimension_semantics=("arbitrary",)),
        cost_estimate=pl.CostEstimate(
            flops=4 * queries.shape[0] * H * TOPN * BLOCK * DH,
            transcendentals=queries.shape[0] * H * TOPN * BLOCK,
            bytes_accessed=2 * queries.size * 2 + query_blocks * TOPN * BLOCK * 2 * DH * 2,
        ),
    )(positions, queries, tile_table)


def solution(mesh):
    placed = (
        P(("pb", "kv"), None),
        P(("kv", "pb"), None),
        P(("kv", "pb"), None),
        P(("pb", "kv"), None),
    )
    return jax.shard_map(
        per_device, mesh=mesh, in_specs=placed, out_specs=P(("pb", "kv"), None), check_vma=False
    )
```

```python
import math

import jax
import jax.numpy as jnp
from jax import lax
from jax.experimental import pallas as pl
from jax.experimental.pallas import tpu as pltpu
from jax.sharding import PartitionSpec as P

H = 8
DH = 128
BLOCK = 64
TOPN = 16
QB = 64
CAP = 2


def holdings(wanted, owner, blocks_here):
    local_ids = owner * blocks_here + jnp.arange(blocks_here, dtype=jnp.int32)
    hits = (wanted[:, None] == local_ids[None, :]).astype(jnp.int32)
    present = jnp.max(hits, axis=0)
    return (present, jnp.cumsum(present) - present)


def slot_lists(present, slot_rank, slots):
    local_ids = jnp.arange(present.shape[-1], dtype=jnp.int32)
    slot_ids = jnp.arange(slots, dtype=jnp.int32)
    matches = (present[..., :, None] == 1) & (slot_rank[..., :, None] == slot_ids)
    return jnp.sum(jnp.where(matches, local_ids[:, None], 0), axis=-2)


def per_device(queries, keys, values, selected):
    pb_count = lax.axis_size("pb")
    kv_count = lax.axis_size("kv")
    devices = pb_count * kv_count
    blocks_here = keys.shape[0] // BLOCK
    query_blocks = queries.shape[0] // QB
    column_blocks = pb_count * blocks_here
    tiles_local = jnp.concatenate(
        [keys.reshape(blocks_here, BLOCK, DH), values.reshape(blocks_here, BLOCK, DH)], axis=2
    )
    column = lax.all_gather(tiles_local, "pb", axis=0, tiled=True)
    slots = CAP
    wanted = selected.reshape(-1)
    owners = jnp.arange(devices, dtype=jnp.int32)
    present, slot_rank = jax.vmap(lambda owner: holdings(wanted, owner, blocks_here))(owners)
    owner_lists = slot_lists(present, slot_rank, slots)
    by_column = owner_lists.reshape(kv_count, pb_count, slots) + (
        jnp.arange(pb_count, dtype=jnp.int32)[None, :, None] * blocks_here
    )
    by_column = by_column.reshape(kv_count, pb_count * slots)
    asked_for = lax.all_to_all(by_column, "kv", split_axis=0, concat_axis=0, tiled=True)
    me_kv = lax.axis_index("kv")
    end_pick = jnp.where(me_kv == kv_count - 1, column_blocks - 1, 0).astype(jnp.int32)
    picks = jnp.concatenate(
        [asked_for.reshape(kv_count, pb_count * slots), jnp.broadcast_to(end_pick, (kv_count, 1))], axis=1
    )
    outgoing = jnp.take(column, picks.reshape(-1), axis=0, mode="clip").reshape(
        kv_count, pb_count * slots + 1, BLOCK, 2 * DH
    )
    fetched = exchange(outgoing)
    tile_table = fetched.reshape(devices * slots + kv_count, BLOCK, 2 * DH)
    owner_of = selected // blocks_here
    positions = owner_of * slots + jnp.take(slot_rank.reshape(-1), selected)
    positions = positions + owner_of // pb_count
    row = pb_count * slots + 1
    leading_positions = jnp.broadcast_to(
        jnp.array([row - 1, kv_count * row - 1], jnp.int32), (query_blocks, 2)
    )
    positions = jnp.concatenate([leading_positions, positions], axis=1)
    positions = jnp.clip(positions, 0, tile_table.shape[0] - 1).reshape(-1)
    return attend_blocks(queries, tile_table, positions)


HEAD_GROUP = 4


SIDE = 4
STEPS = [(dx, dy) for dy in range(SIDE) for dx in range(SIDE) if (dx, dy) != (0, 0)]
DIRECT = [(dx, dy) for (dx, dy) in STEPS if dx != SIDE // 2 and dy != SIDE // 2]
FAR = [(dx, dy) for (dx, dy) in STEPS if dx == SIDE // 2 or dy == SIDE // 2]


RELAY_ROWS = 8


def relays_of(dx, dy):
    if dx == SIDE // 2 and dy == SIDE // 2:
        return [(-1, -1), (1, 1)]
    if dx == SIDE // 2:
        return [(-1, 0), (1, 0)]
    return [(0, -1), (0, 1)]


def exchange_kernel(out_hbm, fetched_hbm, relay_hbm, d_send, d_recv, r_send, r_recv, f_send, f_recv, local_sem):
    rows = out_hbm.shape[1]
    parts = [(0, RELAY_ROWS), (RELAY_ROWS, RELAY_ROWS)]
    far_lo = 2 * RELAY_ROWS
    me = lax.axis_index("kv")
    line = lax.axis_index("pb")
    mx = me % SIDE
    my = me // SIDE

    def at(dx, dy):
        return ((my + dy + SIDE) % SIDE) * SIDE + (mx + dx + SIDE) % SIDE

    def remote(src, dst, send, recv, target):
        return pltpu.make_async_remote_copy(
            src_ref=src, dst_ref=dst, send_sem=send, recv_sem=recv,
            device_id=(line, target), device_id_type=pl.DeviceIdType.MESH,
        )

    barrier = pltpu.get_barrier_semaphore()
    for dx, dy in STEPS:
        pl.semaphore_signal(
            barrier, inc=1, device_id=(line, at(dx, dy)), device_id_type=pl.DeviceIdType.MESH
        )
    pl.semaphore_wait(barrier, len(STEPS))
    local = pltpu.make_async_copy(out_hbm.at[me], fetched_hbm.at[me], local_sem)
    local.start()
    sent = []
    for t, (dx, dy) in enumerate(FAR):
        for h, (rx, ry) in enumerate(relays_of(dx, dy)):
            f = 2 * t + h
            lo, size = parts[h]
            copy = remote(
                out_hbm.at[at(dx, dy), pl.ds(lo, size)], relay_hbm.at[f, pl.ds(0, size)],
                r_send.at[f], r_recv.at[f], at(rx, ry),
            )
            copy.start()
            sent.append(copy)
    for dx, dy in STEPS:
        k = dy * SIDE + dx
        lo = far_lo if (dx, dy) in FAR else 0
        copy = remote(
            out_hbm.at[at(dx, dy), pl.ds(lo, rows - lo)], fetched_hbm.at[me, pl.ds(lo, rows - lo)],
            d_send.at[k], d_recv.at[k], at(dx, dy),
        )
        copy.start()
        sent.append(copy)
    for t, (dx, dy) in enumerate(FAR):
        for h, (rx, ry) in enumerate(relays_of(dx, dy)):
            f = 2 * t + h
            lo, size = parts[h]
            held = relay_hbm.at[f, pl.ds(0, size)]
            remote(held, held, r_send.at[f], r_recv.at[f], at(-rx, -ry)).wait_recv()
            copy = remote(
                held, fetched_hbm.at[at(-rx, -ry), pl.ds(lo, size)],
                f_send.at[f], f_recv.at[f], at(dx - rx, dy - ry),
            )
            copy.start()
            sent.append(copy)
    for copy in sent:
        copy.wait_send()
    for dx, dy in STEPS:
        k = dy * SIDE + dx
        lo = far_lo if (dx, dy) in FAR else 0
        source = at(-dx, -dy)
        part = fetched_hbm.at[source, pl.ds(lo, rows - lo)]
        remote(part, part, d_send.at[k], d_recv.at[k], source).wait_recv()
    for t, (dx, dy) in enumerate(FAR):
        for h in range(2):
            f = 2 * t + h
            lo, size = parts[h]
            source = at(-dx, -dy)
            part = fetched_hbm.at[source, pl.ds(lo, size)]
            remote(part, part, f_send.at[f], f_recv.at[f], source).wait_recv()
    local.wait()


def exchange(outgoing):
    n, rows = outgoing.shape[:2]
    flows = 2 * len(FAR)
    fetched, _ = pl.pallas_call(
        exchange_kernel,
        out_shape=(
            jax.ShapeDtypeStruct(outgoing.shape, outgoing.dtype),
            jax.ShapeDtypeStruct((flows, RELAY_ROWS) + outgoing.shape[2:], outgoing.dtype),
        ),
        in_specs=[pl.BlockSpec(memory_space=pl.ANY)],
        out_specs=(pl.BlockSpec(memory_space=pl.ANY), pl.BlockSpec(memory_space=pl.ANY)),
        scratch_shapes=[
            pltpu.SemaphoreType.DMA((n,)),
            pltpu.SemaphoreType.DMA((n,)),
            pltpu.SemaphoreType.DMA((flows,)),
            pltpu.SemaphoreType.DMA((flows,)),
            pltpu.SemaphoreType.DMA((flows,)),
            pltpu.SemaphoreType.DMA((flows,)),
            pltpu.SemaphoreType.DMA(()),
        ],
        compiler_params=pltpu.CompilerParams(collective_id=0, has_side_effects=True),
    )(outgoing)
    return fetched


def attend_kernel(pos_ref, q_ref, table_hbm, o_ref, kvbuf, sems):
    step = pl.program_id(0)
    steps = pl.num_programs(0)

    def fetch(block, slot):
        for j in range(TOPN):
            pltpu.make_async_copy(
                table_hbm.at[pos_ref[block * TOPN + j]], kvbuf.at[slot, j], sems.at[slot, j]
            ).start()

    @pl.when(step == 0)
    def _():
        fetch(0, 0)

    slot = step % 2

    @pl.when(step + 1 < steps)
    def _():
        fetch(step + 1, 1 - slot)

    for j in range(TOPN):
        pltpu.make_async_copy(table_hbm.at[0], kvbuf.at[slot, j], sems.at[slot, j]).wait()
    tiles = kvbuf[slot]
    k_rows = tiles[:, :, :DH].reshape(TOPN * BLOCK, DH)
    v_rows = tiles[:, :, DH:].reshape(TOPN * BLOCK, DH)
    for g in range(H // HEAD_GROUP):
        heads = range(g * HEAD_GROUP, (g + 1) * HEAD_GROUP)
        q_rows = jnp.concatenate([q_ref[:, h * DH : (h + 1) * DH] for h in heads], axis=0)
        scores = lax.dot_general(
            q_rows, k_rows, (((1,), (1,)), ((), ())), preferred_element_type=jnp.float32
        ) * DH ** (-0.5)
        weights = jnp.exp(scores - jnp.max(scores, axis=-1, keepdims=True))
        totals = jnp.sum(weights, axis=-1, keepdims=True)
        weighted = jnp.dot(
            weights.astype(jnp.bfloat16), v_rows, preferred_element_type=jnp.float32
        )
        out = (weighted / totals).astype(o_ref.dtype)
        for i, h in enumerate(heads):
            o_ref[:, h * DH : (h + 1) * DH] = out[i * QB : (i + 1) * QB]


def attend_blocks(queries, tile_table, positions):
    query_blocks = queries.shape[0] // QB
    return pl.pallas_call(
        attend_kernel,
        out_shape=jax.ShapeDtypeStruct(queries.shape, queries.dtype),
        grid_spec=pltpu.PrefetchScalarGridSpec(
            num_scalar_prefetch=1,
            grid=(query_blocks,),
            in_specs=[
                pl.BlockSpec((QB, H * DH), lambda i, pos: (i, 0)),
                pl.BlockSpec(memory_space=pl.ANY),
            ],
            out_specs=pl.BlockSpec((QB, H * DH), lambda i, pos: (i, 0)),
            scratch_shapes=[
                pltpu.VMEM((2, TOPN, BLOCK, 2 * DH), tile_table.dtype),
                pltpu.SemaphoreType.DMA((2, TOPN)),
            ],
        ),
        compiler_params=pltpu.CompilerParams(dimension_semantics=("arbitrary",)),
        cost_estimate=pl.CostEstimate(
            flops=4 * queries.shape[0] * H * TOPN * BLOCK * DH,
            transcendentals=queries.shape[0] * H * TOPN * BLOCK,
            bytes_accessed=2 * queries.size * 2 + query_blocks * TOPN * BLOCK * 2 * DH * 2,
        ),
    )(positions, queries, tile_table)


def solution(mesh):
    placed = (
        P(("pb", "kv"), None),
        P(("kv", "pb"), None),
        P(("kv", "pb"), None),
        P(("pb", "kv"), None),
    )
    return jax.shard_map(
        per_device, mesh=mesh, in_specs=placed, out_specs=P(("pb", "kv"), None), check_vma=False
    )
```

```python
import math

import jax
import jax.numpy as jnp
from jax import lax
from jax.experimental import pallas as pl
from jax.experimental.pallas import tpu as pltpu
from jax.sharding import PartitionSpec as P

H = 8
DH = 128
BLOCK = 64
TOPN = 16
QB = 64
CAP = 2


def holdings(wanted, owner, blocks_here):
    local_ids = owner * blocks_here + jnp.arange(blocks_here, dtype=jnp.int32)
    hits = (wanted[:, None] == local_ids[None, :]).astype(jnp.int32)
    present = jnp.max(hits, axis=0)
    return (present, jnp.cumsum(present) - present)


def slot_lists(present, slot_rank, slots):
    local_ids = jnp.arange(present.shape[-1], dtype=jnp.int32)
    slot_ids = jnp.arange(slots, dtype=jnp.int32)
    matches = (present[..., :, None] == 1) & (slot_rank[..., :, None] == slot_ids)
    return jnp.sum(jnp.where(matches, local_ids[:, None], 0), axis=-2)


def per_device(queries, keys, values, selected):
    pb_count = lax.axis_size("pb")
    kv_count = lax.axis_size("kv")
    devices = pb_count * kv_count
    blocks_here = keys.shape[0] // BLOCK
    query_blocks = queries.shape[0] // QB
    column_blocks = pb_count * blocks_here
    tiles_local = jnp.concatenate(
        [keys.reshape(blocks_here, BLOCK, DH), values.reshape(blocks_here, BLOCK, DH)], axis=2
    )
    column = lax.all_gather(tiles_local, "pb", axis=0, tiled=True)
    slots = CAP
    wanted = selected.reshape(-1)
    owners = jnp.arange(devices, dtype=jnp.int32)
    present, slot_rank = jax.vmap(lambda owner: holdings(wanted, owner, blocks_here))(owners)
    owner_lists = slot_lists(present, slot_rank, slots)
    by_column = owner_lists.reshape(kv_count, pb_count, slots) + (
        jnp.arange(pb_count, dtype=jnp.int32)[None, :, None] * blocks_here
    )
    by_column = by_column.reshape(kv_count, pb_count * slots)
    asked_for = lax.all_to_all(by_column, "kv", split_axis=0, concat_axis=0, tiled=True)
    me_kv = lax.axis_index("kv")
    end_pick = jnp.where(me_kv == kv_count - 1, column_blocks - 1, 0).astype(jnp.int32)
    picks = jnp.concatenate(
        [asked_for.reshape(kv_count, pb_count * slots), jnp.broadcast_to(end_pick, (kv_count, 1))], axis=1
    )
    outgoing = jnp.take(column, picks.reshape(-1), axis=0, mode="clip").reshape(
        kv_count, pb_count * slots + 1, BLOCK, 2 * DH
    )
    fetched = exchange(outgoing)
    tile_table = fetched.reshape(devices * slots + kv_count, BLOCK, 2 * DH)
    owner_of = selected // blocks_here
    positions = owner_of * slots + jnp.take(slot_rank.reshape(-1), selected)
    positions = positions + owner_of // pb_count
    row = pb_count * slots + 1
    leading_positions = jnp.broadcast_to(
        jnp.array([row - 1, kv_count * row - 1], jnp.int32), (query_blocks, 2)
    )
    positions = jnp.concatenate([leading_positions, positions], axis=1)
    positions = jnp.clip(positions, 0, tile_table.shape[0] - 1).reshape(-1)
    return attend_blocks(queries, tile_table, positions)


HEAD_GROUP = 4


SIDE = 4
STEPS = [(dx, dy) for dy in range(SIDE) for dx in range(SIDE) if (dx, dy) != (0, 0)]
DIRECT = [(dx, dy) for (dx, dy) in STEPS if dx != SIDE // 2 and dy != SIDE // 2]
FAR = [(dx, dy) for (dx, dy) in STEPS if dx == SIDE // 2 or dy == SIDE // 2]


def relays_of(dx, dy):
    if dx == SIDE // 2 and dy == SIDE // 2:
        return [(-1, -1), (1, 1)]
    if dx == SIDE // 2:
        return [(-1, 0), (1, 0)]
    return [(0, -1), (0, 1)]


def exchange_kernel(out_hbm, fetched_hbm, relay_hbm, d_send, d_recv, r_send, r_recv, f_send, f_recv, local_sem):
    rows = out_hbm.shape[1]
    parts = [(0, rows // 2), (rows // 2, rows - rows // 2)]
    me = lax.axis_index("kv")
    line = lax.axis_index("pb")
    mx = me % SIDE
    my = me // SIDE

    def at(dx, dy):
        return ((my + dy + SIDE) % SIDE) * SIDE + (mx + dx + SIDE) % SIDE

    def remote(src, dst, send, recv, target):
        return pltpu.make_async_remote_copy(
            src_ref=src, dst_ref=dst, send_sem=send, recv_sem=recv,
            device_id=(line, target), device_id_type=pl.DeviceIdType.MESH,
        )

    barrier = pltpu.get_barrier_semaphore()
    for dx, dy in STEPS:
        pl.semaphore_signal(
            barrier, inc=1, device_id=(line, at(dx, dy)), device_id_type=pl.DeviceIdType.MESH
        )
    pl.semaphore_wait(barrier, len(STEPS))
    local = pltpu.make_async_copy(out_hbm.at[me], fetched_hbm.at[me], local_sem)
    local.start()
    def chunk(lo, size, c):
        first = size // 2
        return (lo, first) if c == 0 else (lo + first, size - first)

    sent = []
    for c in range(2):
        for t, (dx, dy) in enumerate(FAR):
            for h, (rx, ry) in enumerate(relays_of(dx, dy)):
                f = 2 * t + h
                g = 2 * f + c
                lo, size = parts[h]
                clo, csz = chunk(lo, size, c)
                copy = remote(
                    out_hbm.at[at(dx, dy), pl.ds(clo, csz)], relay_hbm.at[f, pl.ds(clo - lo, csz)],
                    r_send.at[g], r_recv.at[g], at(rx, ry),
                )
                copy.start()
                sent.append(copy)
    for dx, dy in DIRECT:
        k = dy * SIDE + dx
        copy = remote(out_hbm.at[at(dx, dy)], fetched_hbm.at[me], d_send.at[k], d_recv.at[k], at(dx, dy))
        copy.start()
        sent.append(copy)
    for c in range(2):
        for t, (dx, dy) in enumerate(FAR):
            for h, (rx, ry) in enumerate(relays_of(dx, dy)):
                f = 2 * t + h
                g = 2 * f + c
                lo, size = parts[h]
                clo, csz = chunk(lo, size, c)
                held = relay_hbm.at[f, pl.ds(clo - lo, csz)]
                remote(held, held, r_send.at[g], r_recv.at[g], at(-rx, -ry)).wait_recv()
                copy = remote(
                    held, fetched_hbm.at[at(-rx, -ry), pl.ds(clo, csz)],
                    f_send.at[g], f_recv.at[g], at(dx - rx, dy - ry),
                )
                copy.start()
                sent.append(copy)
    for copy in sent:
        copy.wait_send()
    for dx, dy in DIRECT:
        k = dy * SIDE + dx
        source = at(-dx, -dy)
        remote(
            out_hbm.at[source], fetched_hbm.at[source], d_send.at[k], d_recv.at[k], source
        ).wait_recv()
    for t, (dx, dy) in enumerate(FAR):
        for h in range(2):
            f = 2 * t + h
            lo, size = parts[h]
            source = at(-dx, -dy)
            for c in range(2):
                g = 2 * f + c
                clo, csz = chunk(lo, size, c)
                part = fetched_hbm.at[source, pl.ds(clo, csz)]
                remote(part, part, f_send.at[g], f_recv.at[g], source).wait_recv()
    local.wait()


def exchange(outgoing):
    n, rows = outgoing.shape[:2]
    flows = 2 * len(FAR)
    pieces = 2 * flows
    fetched, _ = pl.pallas_call(
        exchange_kernel,
        out_shape=(
            jax.ShapeDtypeStruct(outgoing.shape, outgoing.dtype),
            jax.ShapeDtypeStruct((flows, rows - rows // 2) + outgoing.shape[2:], outgoing.dtype),
        ),
        in_specs=[pl.BlockSpec(memory_space=pl.ANY)],
        out_specs=(pl.BlockSpec(memory_space=pl.ANY), pl.BlockSpec(memory_space=pl.ANY)),
        scratch_shapes=[
            pltpu.SemaphoreType.DMA((n,)),
            pltpu.SemaphoreType.DMA((n,)),
            pltpu.SemaphoreType.DMA((pieces,)),
            pltpu.SemaphoreType.DMA((pieces,)),
            pltpu.SemaphoreType.DMA((pieces,)),
            pltpu.SemaphoreType.DMA((pieces,)),
            pltpu.SemaphoreType.DMA(()),
        ],
        compiler_params=pltpu.CompilerParams(collective_id=0, has_side_effects=True),
    )(outgoing)
    return fetched


def attend_kernel(pos_ref, q_ref, table_hbm, o_ref, kvbuf, sems):
    step = pl.program_id(0)
    steps = pl.num_programs(0)

    def fetch(block, slot):
        for j in range(TOPN):
            pltpu.make_async_copy(
                table_hbm.at[pos_ref[block * TOPN + j]], kvbuf.at[slot, j], sems.at[slot, j]
            ).start()

    @pl.when(step == 0)
    def _():
        fetch(0, 0)

    slot = step % 2

    @pl.when(step + 1 < steps)
    def _():
        fetch(step + 1, 1 - slot)

    for j in range(TOPN):
        pltpu.make_async_copy(table_hbm.at[0], kvbuf.at[slot, j], sems.at[slot, j]).wait()
    tiles = kvbuf[slot]
    k_rows = tiles[:, :, :DH].reshape(TOPN * BLOCK, DH)
    v_rows = tiles[:, :, DH:].reshape(TOPN * BLOCK, DH)
    for g in range(H // HEAD_GROUP):
        heads = range(g * HEAD_GROUP, (g + 1) * HEAD_GROUP)
        q_rows = jnp.concatenate([q_ref[:, h * DH : (h + 1) * DH] for h in heads], axis=0)
        scores = lax.dot_general(
            q_rows, k_rows, (((1,), (1,)), ((), ())), preferred_element_type=jnp.float32
        ) * DH ** (-0.5)
        weights = jnp.exp(scores - jnp.max(scores, axis=-1, keepdims=True))
        totals = jnp.sum(weights, axis=-1, keepdims=True)
        weighted = jnp.dot(
            weights.astype(jnp.bfloat16), v_rows, preferred_element_type=jnp.float32
        )
        out = (weighted / totals).astype(o_ref.dtype)
        for i, h in enumerate(heads):
            o_ref[:, h * DH : (h + 1) * DH] = out[i * QB : (i + 1) * QB]


def attend_blocks(queries, tile_table, positions):
    query_blocks = queries.shape[0] // QB
    return pl.pallas_call(
        attend_kernel,
        out_shape=jax.ShapeDtypeStruct(queries.shape, queries.dtype),
        grid_spec=pltpu.PrefetchScalarGridSpec(
            num_scalar_prefetch=1,
            grid=(query_blocks,),
            in_specs=[
                pl.BlockSpec((QB, H * DH), lambda i, pos: (i, 0)),
                pl.BlockSpec(memory_space=pl.ANY),
            ],
            out_specs=pl.BlockSpec((QB, H * DH), lambda i, pos: (i, 0)),
            scratch_shapes=[
                pltpu.VMEM((2, TOPN, BLOCK, 2 * DH), tile_table.dtype),
                pltpu.SemaphoreType.DMA((2, TOPN)),
            ],
        ),
        compiler_params=pltpu.CompilerParams(dimension_semantics=("arbitrary",)),
        cost_estimate=pl.CostEstimate(
            flops=4 * queries.shape[0] * H * TOPN * BLOCK * DH,
            transcendentals=queries.shape[0] * H * TOPN * BLOCK,
            bytes_accessed=2 * queries.size * 2 + query_blocks * TOPN * BLOCK * 2 * DH * 2,
        ),
    )(positions, queries, tile_table)


def solution(mesh):
    placed = (
        P(("pb", "kv"), None),
        P(("kv", "pb"), None),
        P(("kv", "pb"), None),
        P(("pb", "kv"), None),
    )
    return jax.shard_map(
        per_device, mesh=mesh, in_specs=placed, out_specs=P(("pb", "kv"), None), check_vma=False
    )
```

```python
import math

import jax
import jax.numpy as jnp
from jax import lax
from jax.experimental import pallas as pl
from jax.experimental.pallas import tpu as pltpu
from jax.sharding import PartitionSpec as P

H = 8
DH = 128
BLOCK = 64
TOPN = 16
QB = 64
CAP = 2


def holdings(wanted, owner, blocks_here):
    local_ids = owner * blocks_here + jnp.arange(blocks_here, dtype=jnp.int32)
    hits = (wanted[:, None] == local_ids[None, :]).astype(jnp.int32)
    present = jnp.max(hits, axis=0)
    return (present, jnp.cumsum(present) - present)


def slot_lists(present, slot_rank, slots):
    local_ids = jnp.arange(present.shape[-1], dtype=jnp.int32)
    slot_ids = jnp.arange(slots, dtype=jnp.int32)
    matches = (present[..., :, None] == 1) & (slot_rank[..., :, None] == slot_ids)
    return jnp.sum(jnp.where(matches, local_ids[:, None], 0), axis=-2)


def per_device(queries, keys, values, selected):
    pb_count = lax.axis_size("pb")
    kv_count = lax.axis_size("kv")
    devices = pb_count * kv_count
    blocks_here = keys.shape[0] // BLOCK
    query_blocks = queries.shape[0] // QB
    column_blocks = pb_count * blocks_here
    tiles_local = jnp.concatenate(
        [keys.reshape(blocks_here, BLOCK, DH), values.reshape(blocks_here, BLOCK, DH)], axis=2
    )
    column = lax.all_gather(tiles_local, "pb", axis=0, tiled=True)
    slots = CAP
    wanted = selected.reshape(-1)
    owners = jnp.arange(devices, dtype=jnp.int32)
    present, slot_rank = jax.vmap(lambda owner: holdings(wanted, owner, blocks_here))(owners)
    owner_lists = slot_lists(present, slot_rank, slots)
    by_column = owner_lists.reshape(kv_count, pb_count, slots) + (
        jnp.arange(pb_count, dtype=jnp.int32)[None, :, None] * blocks_here
    )
    by_column = by_column.reshape(kv_count, pb_count * slots)
    asked_for = lax.all_to_all(by_column, "kv", split_axis=0, concat_axis=0, tiled=True)
    me_kv = lax.axis_index("kv")
    end_pick = jnp.where(me_kv == kv_count - 1, column_blocks - 1, 0).astype(jnp.int32)
    picks = jnp.concatenate(
        [asked_for.reshape(kv_count, pb_count * slots), jnp.broadcast_to(end_pick, (kv_count, 1))], axis=1
    )
    outgoing = jnp.take(column, picks.reshape(-1), axis=0, mode="clip").reshape(
        kv_count, pb_count * slots + 1, BLOCK, 2 * DH
    )
    fetched = exchange(outgoing)
    tile_table = fetched.reshape(devices * slots + kv_count, BLOCK, 2 * DH)
    owner_of = selected // blocks_here
    positions = owner_of * slots + jnp.take(slot_rank.reshape(-1), selected)
    positions = positions + owner_of // pb_count
    row = pb_count * slots + 1
    leading_positions = jnp.broadcast_to(
        jnp.array([row - 1, kv_count * row - 1], jnp.int32), (query_blocks, 2)
    )
    positions = jnp.concatenate([leading_positions, positions], axis=1)
    positions = jnp.clip(positions, 0, tile_table.shape[0] - 1).reshape(-1)
    return attend_blocks(queries, tile_table, positions)


HEAD_GROUP = 4


SIDE = 4
STEPS = [(dx, dy) for dy in range(SIDE) for dx in range(SIDE) if (dx, dy) != (0, 0)]
DIRECT = [(dx, dy) for (dx, dy) in STEPS if dx != SIDE // 2 and dy != SIDE // 2]
FAR = [(dx, dy) for (dx, dy) in STEPS if dx == SIDE // 2 or dy == SIDE // 2]


CHUNKS = 4


def relays_of(dx, dy):
    if dx == SIDE // 2 and dy == SIDE // 2:
        return [(-1, -1), (1, 1)]
    if dx == SIDE // 2:
        return [(-1, 0), (1, 0)]
    return [(0, -1), (0, 1)]


def exchange_kernel(out_hbm, fetched_hbm, relay_hbm, d_send, d_recv, r_send, r_recv, f_send, f_recv, local_sem):
    rows = out_hbm.shape[1]
    parts = [(0, rows // 2), (rows // 2, rows - rows // 2)]
    me = lax.axis_index("kv")
    line = lax.axis_index("pb")
    mx = me % SIDE
    my = me // SIDE

    def at(dx, dy):
        return ((my + dy + SIDE) % SIDE) * SIDE + (mx + dx + SIDE) % SIDE

    def remote(src, dst, send, recv, target):
        return pltpu.make_async_remote_copy(
            src_ref=src, dst_ref=dst, send_sem=send, recv_sem=recv,
            device_id=(line, target), device_id_type=pl.DeviceIdType.MESH,
        )

    barrier = pltpu.get_barrier_semaphore()
    for dx, dy in STEPS:
        pl.semaphore_signal(
            barrier, inc=1, device_id=(line, at(dx, dy)), device_id_type=pl.DeviceIdType.MESH
        )
    pl.semaphore_wait(barrier, len(STEPS))
    local = pltpu.make_async_copy(out_hbm.at[me], fetched_hbm.at[me], local_sem)
    local.start()
    def chunk(lo, size, c):
        step = size // CHUNKS
        return (lo + c * step, step if c < CHUNKS - 1 else size - (CHUNKS - 1) * step)

    sent = []
    for c in range(CHUNKS):
        for t, (dx, dy) in enumerate(FAR):
            for h, (rx, ry) in enumerate(relays_of(dx, dy)):
                f = 2 * t + h
                g = CHUNKS * f + c
                lo, size = parts[h]
                clo, csz = chunk(lo, size, c)
                copy = remote(
                    out_hbm.at[at(dx, dy), pl.ds(clo, csz)], relay_hbm.at[f, pl.ds(clo - lo, csz)],
                    r_send.at[g], r_recv.at[g], at(rx, ry),
                )
                copy.start()
                sent.append(copy)
    for dx, dy in DIRECT:
        k = dy * SIDE + dx
        copy = remote(out_hbm.at[at(dx, dy)], fetched_hbm.at[me], d_send.at[k], d_recv.at[k], at(dx, dy))
        copy.start()
        sent.append(copy)
    for c in range(CHUNKS):
        for t, (dx, dy) in enumerate(FAR):
            for h, (rx, ry) in enumerate(relays_of(dx, dy)):
                f = 2 * t + h
                g = CHUNKS * f + c
                lo, size = parts[h]
                clo, csz = chunk(lo, size, c)
                held = relay_hbm.at[f, pl.ds(clo - lo, csz)]
                remote(held, held, r_send.at[g], r_recv.at[g], at(-rx, -ry)).wait_recv()
                copy = remote(
                    held, fetched_hbm.at[at(-rx, -ry), pl.ds(clo, csz)],
                    f_send.at[g], f_recv.at[g], at(dx - rx, dy - ry),
                )
                copy.start()
                sent.append(copy)
    for copy in sent:
        copy.wait_send()
    for dx, dy in DIRECT:
        k = dy * SIDE + dx
        source = at(-dx, -dy)
        remote(
            out_hbm.at[source], fetched_hbm.at[source], d_send.at[k], d_recv.at[k], source
        ).wait_recv()
    for t, (dx, dy) in enumerate(FAR):
        for h in range(2):
            f = 2 * t + h
            lo, size = parts[h]
            source = at(-dx, -dy)
            for c in range(CHUNKS):
                g = CHUNKS * f + c
                clo, csz = chunk(lo, size, c)
                part = fetched_hbm.at[source, pl.ds(clo, csz)]
                remote(part, part, f_send.at[g], f_recv.at[g], source).wait_recv()
    local.wait()


def exchange(outgoing):
    n, rows = outgoing.shape[:2]
    flows = 2 * len(FAR)
    pieces = CHUNKS * flows
    fetched, _ = pl.pallas_call(
        exchange_kernel,
        out_shape=(
            jax.ShapeDtypeStruct(outgoing.shape, outgoing.dtype),
            jax.ShapeDtypeStruct((flows, rows - rows // 2) + outgoing.shape[2:], outgoing.dtype),
        ),
        in_specs=[pl.BlockSpec(memory_space=pl.ANY)],
        out_specs=(pl.BlockSpec(memory_space=pl.ANY), pl.BlockSpec(memory_space=pl.ANY)),
        scratch_shapes=[
            pltpu.SemaphoreType.DMA((n,)),
            pltpu.SemaphoreType.DMA((n,)),
            pltpu.SemaphoreType.DMA((pieces,)),
            pltpu.SemaphoreType.DMA((pieces,)),
            pltpu.SemaphoreType.DMA((pieces,)),
            pltpu.SemaphoreType.DMA((pieces,)),
            pltpu.SemaphoreType.DMA(()),
        ],
        compiler_params=pltpu.CompilerParams(collective_id=0, has_side_effects=True),
    )(outgoing)
    return fetched


def attend_kernel(pos_ref, q_ref, table_hbm, o_ref, kvbuf, sems):
    step = pl.program_id(0)
    steps = pl.num_programs(0)

    def fetch(block, slot):
        for j in range(TOPN):
            pltpu.make_async_copy(
                table_hbm.at[pos_ref[block * TOPN + j]], kvbuf.at[slot, j], sems.at[slot, j]
            ).start()

    @pl.when(step == 0)
    def _():
        fetch(0, 0)

    slot = step % 2

    @pl.when(step + 1 < steps)
    def _():
        fetch(step + 1, 1 - slot)

    for j in range(TOPN):
        pltpu.make_async_copy(table_hbm.at[0], kvbuf.at[slot, j], sems.at[slot, j]).wait()
    tiles = kvbuf[slot]
    k_rows = tiles[:, :, :DH].reshape(TOPN * BLOCK, DH)
    v_rows = tiles[:, :, DH:].reshape(TOPN * BLOCK, DH)
    for g in range(H // HEAD_GROUP):
        heads = range(g * HEAD_GROUP, (g + 1) * HEAD_GROUP)
        q_rows = jnp.concatenate([q_ref[:, h * DH : (h + 1) * DH] for h in heads], axis=0)
        scores = lax.dot_general(
            q_rows, k_rows, (((1,), (1,)), ((), ())), preferred_element_type=jnp.float32
        ) * DH ** (-0.5)
        weights = jnp.exp(scores - jnp.max(scores, axis=-1, keepdims=True))
        totals = jnp.sum(weights, axis=-1, keepdims=True)
        weighted = jnp.dot(
            weights.astype(jnp.bfloat16), v_rows, preferred_element_type=jnp.float32
        )
        out = (weighted / totals).astype(o_ref.dtype)
        for i, h in enumerate(heads):
            o_ref[:, h * DH : (h + 1) * DH] = out[i * QB : (i + 1) * QB]


def attend_blocks(queries, tile_table, positions):
    query_blocks = queries.shape[0] // QB
    return pl.pallas_call(
        attend_kernel,
        out_shape=jax.ShapeDtypeStruct(queries.shape, queries.dtype),
        grid_spec=pltpu.PrefetchScalarGridSpec(
            num_scalar_prefetch=1,
            grid=(query_blocks,),
            in_specs=[
                pl.BlockSpec((QB, H * DH), lambda i, pos: (i, 0)),
                pl.BlockSpec(memory_space=pl.ANY),
            ],
            out_specs=pl.BlockSpec((QB, H * DH), lambda i, pos: (i, 0)),
            scratch_shapes=[
                pltpu.VMEM((2, TOPN, BLOCK, 2 * DH), tile_table.dtype),
                pltpu.SemaphoreType.DMA((2, TOPN)),
            ],
        ),
        compiler_params=pltpu.CompilerParams(dimension_semantics=("arbitrary",)),
        cost_estimate=pl.CostEstimate(
            flops=4 * queries.shape[0] * H * TOPN * BLOCK * DH,
            transcendentals=queries.shape[0] * H * TOPN * BLOCK,
            bytes_accessed=2 * queries.size * 2 + query_blocks * TOPN * BLOCK * 2 * DH * 2,
        ),
    )(positions, queries, tile_table)


def solution(mesh):
    placed = (
        P(("pb", "kv"), None),
        P(("kv", "pb"), None),
        P(("kv", "pb"), None),
        P(("pb", "kv"), None),
    )
    return jax.shard_map(
        per_device, mesh=mesh, in_specs=placed, out_specs=P(("pb", "kv"), None), check_vma=False
    )
```

```python
import math

import jax
import jax.numpy as jnp
from jax import lax
from jax.experimental import pallas as pl
from jax.experimental.pallas import tpu as pltpu
from jax.sharding import PartitionSpec as P

H = 8
DH = 128
BLOCK = 64
TOPN = 16
QB = 64
CAP = 2


def holdings(wanted, owner, blocks_here):
    local_ids = owner * blocks_here + jnp.arange(blocks_here, dtype=jnp.int32)
    hits = (wanted[:, None] == local_ids[None, :]).astype(jnp.int32)
    present = jnp.max(hits, axis=0)
    return (present, jnp.cumsum(present) - present)


def slot_lists(present, slot_rank, slots):
    local_ids = jnp.arange(present.shape[-1], dtype=jnp.int32)
    slot_ids = jnp.arange(slots, dtype=jnp.int32)
    matches = (present[..., :, None] == 1) & (slot_rank[..., :, None] == slot_ids)
    return jnp.sum(jnp.where(matches, local_ids[:, None], 0), axis=-2)


def per_device(queries, keys, values, selected):
    pb_count = lax.axis_size("pb")
    kv_count = lax.axis_size("kv")
    devices = pb_count * kv_count
    blocks_here = keys.shape[0] // BLOCK
    query_blocks = queries.shape[0] // QB
    column_blocks = pb_count * blocks_here
    tiles_local = jnp.concatenate(
        [keys.reshape(blocks_here, BLOCK, DH), values.reshape(blocks_here, BLOCK, DH)], axis=2
    )
    column = lax.all_gather(tiles_local, "pb", axis=0, tiled=True)
    slots = CAP
    wanted = selected.reshape(-1)
    owners = jnp.arange(devices, dtype=jnp.int32)
    present, slot_rank = jax.vmap(lambda owner: holdings(wanted, owner, blocks_here))(owners)
    owner_lists = slot_lists(present, slot_rank, slots)
    by_column = owner_lists.reshape(kv_count, pb_count, slots) + (
        jnp.arange(pb_count, dtype=jnp.int32)[None, :, None] * blocks_here
    )
    by_column = by_column.reshape(kv_count, pb_count * slots)
    asked_for = lax.all_to_all(by_column, "kv", split_axis=0, concat_axis=0, tiled=True)
    me_kv = lax.axis_index("kv")
    end_pick = jnp.where(me_kv == kv_count - 1, column_blocks - 1, 0).astype(jnp.int32)
    picks = jnp.concatenate(
        [asked_for.reshape(kv_count, pb_count * slots), jnp.broadcast_to(end_pick, (kv_count, 1))], axis=1
    )
    outgoing = jnp.take(column, picks.reshape(-1), axis=0, mode="clip").reshape(
        kv_count, pb_count * slots + 1, BLOCK, 2 * DH
    )
    fetched = exchange(outgoing)
    tile_table = fetched.reshape(devices * slots + kv_count, BLOCK, 2 * DH)
    owner_of = selected // blocks_here
    positions = owner_of * slots + jnp.take(slot_rank.reshape(-1), selected)
    positions = positions + owner_of // pb_count
    row = pb_count * slots + 1
    leading_positions = jnp.broadcast_to(
        jnp.array([row - 1, kv_count * row - 1], jnp.int32), (query_blocks, 2)
    )
    positions = jnp.concatenate([leading_positions, positions], axis=1)
    positions = jnp.clip(positions, 0, tile_table.shape[0] - 1).reshape(-1)
    return attend_blocks(queries, tile_table, positions)


HEAD_GROUP = 4


SIDE = 4
STEPS = [(dx, dy) for dy in range(SIDE) for dx in range(SIDE) if (dx, dy) != (0, 0)]
DIRECT = [(dx, dy) for (dx, dy) in STEPS if dx != SIDE // 2 and dy != SIDE // 2]
FAR = [(dx, dy) for (dx, dy) in STEPS if dx == SIDE // 2 or dy == SIDE // 2]


CHUNKS = 8


def relays_of(dx, dy):
    if dx == SIDE // 2 and dy == SIDE // 2:
        return [(-1, -1), (1, 1)]
    if dx == SIDE // 2:
        return [(-1, 0), (1, 0)]
    return [(0, -1), (0, 1)]


def exchange_kernel(out_hbm, fetched_hbm, relay_hbm, d_send, d_recv, r_send, r_recv, f_send, f_recv, local_sem):
    rows = out_hbm.shape[1]
    parts = [(0, rows // 2), (rows // 2, rows - rows // 2)]
    me = lax.axis_index("kv")
    line = lax.axis_index("pb")
    mx = me % SIDE
    my = me // SIDE

    def at(dx, dy):
        return ((my + dy + SIDE) % SIDE) * SIDE + (mx + dx + SIDE) % SIDE

    def remote(src, dst, send, recv, target):
        return pltpu.make_async_remote_copy(
            src_ref=src, dst_ref=dst, send_sem=send, recv_sem=recv,
            device_id=(line, target), device_id_type=pl.DeviceIdType.MESH,
        )

    barrier = pltpu.get_barrier_semaphore()
    for dx, dy in STEPS:
        pl.semaphore_signal(
            barrier, inc=1, device_id=(line, at(dx, dy)), device_id_type=pl.DeviceIdType.MESH
        )
    pl.semaphore_wait(barrier, len(STEPS))
    local = pltpu.make_async_copy(out_hbm.at[me], fetched_hbm.at[me], local_sem)
    local.start()
    def chunk(lo, size, c):
        step = size // CHUNKS
        return (lo + c * step, step if c < CHUNKS - 1 else size - (CHUNKS - 1) * step)

    sent = []
    for c in range(CHUNKS):
        for t, (dx, dy) in enumerate(FAR):
            for h, (rx, ry) in enumerate(relays_of(dx, dy)):
                f = 2 * t + h
                g = CHUNKS * f + c
                lo, size = parts[h]
                clo, csz = chunk(lo, size, c)
                copy = remote(
                    out_hbm.at[at(dx, dy), pl.ds(clo, csz)], relay_hbm.at[f, pl.ds(clo - lo, csz)],
                    r_send.at[g], r_recv.at[g], at(rx, ry),
                )
                copy.start()
                sent.append(copy)
    for dx, dy in DIRECT:
        k = dy * SIDE + dx
        copy = remote(out_hbm.at[at(dx, dy)], fetched_hbm.at[me], d_send.at[k], d_recv.at[k], at(dx, dy))
        copy.start()
        sent.append(copy)
    for c in range(CHUNKS):
        for t, (dx, dy) in enumerate(FAR):
            for h, (rx, ry) in enumerate(relays_of(dx, dy)):
                f = 2 * t + h
                g = CHUNKS * f + c
                lo, size = parts[h]
                clo, csz = chunk(lo, size, c)
                held = relay_hbm.at[f, pl.ds(clo - lo, csz)]
                remote(held, held, r_send.at[g], r_recv.at[g], at(-rx, -ry)).wait_recv()
                copy = remote(
                    held, fetched_hbm.at[at(-rx, -ry), pl.ds(clo, csz)],
                    f_send.at[g], f_recv.at[g], at(dx - rx, dy - ry),
                )
                copy.start()
                sent.append(copy)
    for copy in sent:
        copy.wait_send()
    for dx, dy in DIRECT:
        k = dy * SIDE + dx
        source = at(-dx, -dy)
        remote(
            out_hbm.at[source], fetched_hbm.at[source], d_send.at[k], d_recv.at[k], source
        ).wait_recv()
    for t, (dx, dy) in enumerate(FAR):
        for h in range(2):
            f = 2 * t + h
            lo, size = parts[h]
            source = at(-dx, -dy)
            for c in range(CHUNKS):
                g = CHUNKS * f + c
                clo, csz = chunk(lo, size, c)
                part = fetched_hbm.at[source, pl.ds(clo, csz)]
                remote(part, part, f_send.at[g], f_recv.at[g], source).wait_recv()
    local.wait()


def exchange(outgoing):
    n, rows = outgoing.shape[:2]
    flows = 2 * len(FAR)
    pieces = CHUNKS * flows
    fetched, _ = pl.pallas_call(
        exchange_kernel,
        out_shape=(
            jax.ShapeDtypeStruct(outgoing.shape, outgoing.dtype),
            jax.ShapeDtypeStruct((flows, rows - rows // 2) + outgoing.shape[2:], outgoing.dtype),
        ),
        in_specs=[pl.BlockSpec(memory_space=pl.ANY)],
        out_specs=(pl.BlockSpec(memory_space=pl.ANY), pl.BlockSpec(memory_space=pl.ANY)),
        scratch_shapes=[
            pltpu.SemaphoreType.DMA((n,)),
            pltpu.SemaphoreType.DMA((n,)),
            pltpu.SemaphoreType.DMA((pieces,)),
            pltpu.SemaphoreType.DMA((pieces,)),
            pltpu.SemaphoreType.DMA((pieces,)),
            pltpu.SemaphoreType.DMA((pieces,)),
            pltpu.SemaphoreType.DMA(()),
        ],
        compiler_params=pltpu.CompilerParams(collective_id=0, has_side_effects=True),
    )(outgoing)
    return fetched


def attend_kernel(pos_ref, q_ref, table_hbm, o_ref, kvbuf, sems):
    step = pl.program_id(0)
    steps = pl.num_programs(0)

    def fetch(block, slot):
        for j in range(TOPN):
            pltpu.make_async_copy(
                table_hbm.at[pos_ref[block * TOPN + j]], kvbuf.at[slot, j], sems.at[slot, j]
            ).start()

    @pl.when(step == 0)
    def _():
        fetch(0, 0)

    slot = step % 2

    @pl.when(step + 1 < steps)
    def _():
        fetch(step + 1, 1 - slot)

    for j in range(TOPN):
        pltpu.make_async_copy(table_hbm.at[0], kvbuf.at[slot, j], sems.at[slot, j]).wait()
    tiles = kvbuf[slot]
    k_rows = tiles[:, :, :DH].reshape(TOPN * BLOCK, DH)
    v_rows = tiles[:, :, DH:].reshape(TOPN * BLOCK, DH)
    for g in range(H // HEAD_GROUP):
        heads = range(g * HEAD_GROUP, (g + 1) * HEAD_GROUP)
        q_rows = jnp.concatenate([q_ref[:, h * DH : (h + 1) * DH] for h in heads], axis=0)
        scores = lax.dot_general(
            q_rows, k_rows, (((1,), (1,)), ((), ())), preferred_element_type=jnp.float32
        ) * DH ** (-0.5)
        weights = jnp.exp(scores - jnp.max(scores, axis=-1, keepdims=True))
        totals = jnp.sum(weights, axis=-1, keepdims=True)
        weighted = jnp.dot(
            weights.astype(jnp.bfloat16), v_rows, preferred_element_type=jnp.float32
        )
        out = (weighted / totals).astype(o_ref.dtype)
        for i, h in enumerate(heads):
            o_ref[:, h * DH : (h + 1) * DH] = out[i * QB : (i + 1) * QB]


def attend_blocks(queries, tile_table, positions):
    query_blocks = queries.shape[0] // QB
    return pl.pallas_call(
        attend_kernel,
        out_shape=jax.ShapeDtypeStruct(queries.shape, queries.dtype),
        grid_spec=pltpu.PrefetchScalarGridSpec(
            num_scalar_prefetch=1,
            grid=(query_blocks,),
            in_specs=[
                pl.BlockSpec((QB, H * DH), lambda i, pos: (i, 0)),
                pl.BlockSpec(memory_space=pl.ANY),
            ],
            out_specs=pl.BlockSpec((QB, H * DH), lambda i, pos: (i, 0)),
            scratch_shapes=[
                pltpu.VMEM((2, TOPN, BLOCK, 2 * DH), tile_table.dtype),
                pltpu.SemaphoreType.DMA((2, TOPN)),
            ],
        ),
        compiler_params=pltpu.CompilerParams(dimension_semantics=("arbitrary",)),
        cost_estimate=pl.CostEstimate(
            flops=4 * queries.shape[0] * H * TOPN * BLOCK * DH,
            transcendentals=queries.shape[0] * H * TOPN * BLOCK,
            bytes_accessed=2 * queries.size * 2 + query_blocks * TOPN * BLOCK * 2 * DH * 2,
        ),
    )(positions, queries, tile_table)


def solution(mesh):
    placed = (
        P(("pb", "kv"), None),
        P(("kv", "pb"), None),
        P(("kv", "pb"), None),
        P(("pb", "kv"), None),
    )
    return jax.shard_map(
        per_device, mesh=mesh, in_specs=placed, out_specs=P(("pb", "kv"), None), check_vma=False
    )
```

```python
import math

import jax
import jax.numpy as jnp
from jax import lax
from jax.experimental import pallas as pl
from jax.experimental.pallas import tpu as pltpu
from jax.sharding import PartitionSpec as P

H = 8
DH = 128
BLOCK = 64
TOPN = 16
QB = 64
CAP = 2


def holdings(wanted, owner, blocks_here):
    local_ids = owner * blocks_here + jnp.arange(blocks_here, dtype=jnp.int32)
    hits = (wanted[:, None] == local_ids[None, :]).astype(jnp.int32)
    present = jnp.max(hits, axis=0)
    return (present, jnp.cumsum(present) - present)


def slot_lists(present, slot_rank, slots):
    local_ids = jnp.arange(present.shape[-1], dtype=jnp.int32)
    slot_ids = jnp.arange(slots, dtype=jnp.int32)
    matches = (present[..., :, None] == 1) & (slot_rank[..., :, None] == slot_ids)
    return jnp.sum(jnp.where(matches, local_ids[:, None], 0), axis=-2)


def per_device(queries, keys, values, selected):
    pb_count = lax.axis_size("pb")
    kv_count = lax.axis_size("kv")
    devices = pb_count * kv_count
    blocks_here = keys.shape[0] // BLOCK
    query_blocks = queries.shape[0] // QB
    column_blocks = pb_count * blocks_here
    tiles_local = jnp.concatenate(
        [keys.reshape(blocks_here, BLOCK, DH), values.reshape(blocks_here, BLOCK, DH)], axis=2
    )
    column = lax.all_gather(tiles_local, "pb", axis=0, tiled=True)
    slots = CAP
    wanted = selected.reshape(-1)
    owners = jnp.arange(devices, dtype=jnp.int32)
    present, slot_rank = jax.vmap(lambda owner: holdings(wanted, owner, blocks_here))(owners)
    owner_lists = slot_lists(present, slot_rank, slots)
    by_column = owner_lists.reshape(kv_count, pb_count, slots) + (
        jnp.arange(pb_count, dtype=jnp.int32)[None, :, None] * blocks_here
    )
    by_column = by_column.reshape(kv_count, pb_count * slots)
    asked_for = lax.all_to_all(by_column, "kv", split_axis=0, concat_axis=0, tiled=True)
    me_kv = lax.axis_index("kv")
    end_pick = jnp.where(me_kv == kv_count - 1, column_blocks - 1, 0).astype(jnp.int32)
    picks = jnp.concatenate(
        [asked_for.reshape(kv_count, pb_count * slots), jnp.broadcast_to(end_pick, (kv_count, 1))], axis=1
    )
    outgoing = jnp.take(column, picks.reshape(-1), axis=0, mode="clip").reshape(
        kv_count, pb_count * slots + 1, BLOCK, 2 * DH
    )
    fetched = exchange(outgoing)
    tile_table = fetched.reshape(devices * slots + kv_count, BLOCK, 2 * DH)
    owner_of = selected // blocks_here
    positions = owner_of * slots + jnp.take(slot_rank.reshape(-1), selected)
    positions = positions + owner_of // pb_count
    row = pb_count * slots + 1
    leading_positions = jnp.broadcast_to(
        jnp.array([row - 1, kv_count * row - 1], jnp.int32), (query_blocks, 2)
    )
    positions = jnp.concatenate([leading_positions, positions], axis=1)
    positions = jnp.clip(positions, 0, tile_table.shape[0] - 1).reshape(-1)
    return attend_blocks(queries, tile_table, positions)


HEAD_GROUP = 4


SIDE = 4
STEPS = [(dx, dy) for dy in range(SIDE) for dx in range(SIDE) if (dx, dy) != (0, 0)]
DIRECT = [(dx, dy) for (dx, dy) in STEPS if dx != SIDE // 2 and dy != SIDE // 2]
FAR = [(dx, dy) for (dx, dy) in STEPS if dx == SIDE // 2 or dy == SIDE // 2]


CHUNKS = 6


def relays_of(dx, dy):
    if dx == SIDE // 2 and dy == SIDE // 2:
        return [(-1, -1), (1, 1)]
    if dx == SIDE // 2:
        return [(-1, 0), (1, 0)]
    return [(0, -1), (0, 1)]


def exchange_kernel(out_hbm, fetched_hbm, relay_hbm, d_send, d_recv, r_send, r_recv, f_send, f_recv, local_sem):
    rows = out_hbm.shape[1]
    parts = [(0, rows // 2), (rows // 2, rows - rows // 2)]
    me = lax.axis_index("kv")
    line = lax.axis_index("pb")
    mx = me % SIDE
    my = me // SIDE

    def at(dx, dy):
        return ((my + dy + SIDE) % SIDE) * SIDE + (mx + dx + SIDE) % SIDE

    def remote(src, dst, send, recv, target):
        return pltpu.make_async_remote_copy(
            src_ref=src, dst_ref=dst, send_sem=send, recv_sem=recv,
            device_id=(line, target), device_id_type=pl.DeviceIdType.MESH,
        )

    barrier = pltpu.get_barrier_semaphore()
    for dx, dy in STEPS:
        pl.semaphore_signal(
            barrier, inc=1, device_id=(line, at(dx, dy)), device_id_type=pl.DeviceIdType.MESH
        )
    pl.semaphore_wait(barrier, len(STEPS))
    local = pltpu.make_async_copy(out_hbm.at[me], fetched_hbm.at[me], local_sem)
    local.start()
    def chunk(lo, size, c):
        step = size // CHUNKS
        return (lo + c * step, step if c < CHUNKS - 1 else size - (CHUNKS - 1) * step)

    sent = []
    for c in range(CHUNKS):
        for t, (dx, dy) in enumerate(FAR):
            for h, (rx, ry) in enumerate(relays_of(dx, dy)):
                f = 2 * t + h
                g = CHUNKS * f + c
                lo, size = parts[h]
                clo, csz = chunk(lo, size, c)
                copy = remote(
                    out_hbm.at[at(dx, dy), pl.ds(clo, csz)], relay_hbm.at[f, pl.ds(clo - lo, csz)],
                    r_send.at[g], r_recv.at[g], at(rx, ry),
                )
                copy.start()
                sent.append(copy)
    for dx, dy in DIRECT:
        k = dy * SIDE + dx
        copy = remote(out_hbm.at[at(dx, dy)], fetched_hbm.at[me], d_send.at[k], d_recv.at[k], at(dx, dy))
        copy.start()
        sent.append(copy)
    for c in range(CHUNKS):
        for t, (dx, dy) in enumerate(FAR):
            for h, (rx, ry) in enumerate(relays_of(dx, dy)):
                f = 2 * t + h
                g = CHUNKS * f + c
                lo, size = parts[h]
                clo, csz = chunk(lo, size, c)
                held = relay_hbm.at[f, pl.ds(clo - lo, csz)]
                remote(held, held, r_send.at[g], r_recv.at[g], at(-rx, -ry)).wait_recv()
                copy = remote(
                    held, fetched_hbm.at[at(-rx, -ry), pl.ds(clo, csz)],
                    f_send.at[g], f_recv.at[g], at(dx - rx, dy - ry),
                )
                copy.start()
                sent.append(copy)
    for copy in sent:
        copy.wait_send()
    for dx, dy in DIRECT:
        k = dy * SIDE + dx
        source = at(-dx, -dy)
        remote(
            out_hbm.at[source], fetched_hbm.at[source], d_send.at[k], d_recv.at[k], source
        ).wait_recv()
    for t, (dx, dy) in enumerate(FAR):
        for h in range(2):
            f = 2 * t + h
            lo, size = parts[h]
            source = at(-dx, -dy)
            for c in range(CHUNKS):
                g = CHUNKS * f + c
                clo, csz = chunk(lo, size, c)
                part = fetched_hbm.at[source, pl.ds(clo, csz)]
                remote(part, part, f_send.at[g], f_recv.at[g], source).wait_recv()
    local.wait()


def exchange(outgoing):
    n, rows = outgoing.shape[:2]
    flows = 2 * len(FAR)
    pieces = CHUNKS * flows
    fetched, _ = pl.pallas_call(
        exchange_kernel,
        out_shape=(
            jax.ShapeDtypeStruct(outgoing.shape, outgoing.dtype),
            jax.ShapeDtypeStruct((flows, rows - rows // 2) + outgoing.shape[2:], outgoing.dtype),
        ),
        in_specs=[pl.BlockSpec(memory_space=pl.ANY)],
        out_specs=(pl.BlockSpec(memory_space=pl.ANY), pl.BlockSpec(memory_space=pl.ANY)),
        scratch_shapes=[
            pltpu.SemaphoreType.DMA((n,)),
            pltpu.SemaphoreType.DMA((n,)),
            pltpu.SemaphoreType.DMA((pieces,)),
            pltpu.SemaphoreType.DMA((pieces,)),
            pltpu.SemaphoreType.DMA((pieces,)),
            pltpu.SemaphoreType.DMA((pieces,)),
            pltpu.SemaphoreType.DMA(()),
        ],
        compiler_params=pltpu.CompilerParams(collective_id=0, has_side_effects=True),
    )(outgoing)
    return fetched


def attend_kernel(pos_ref, q_ref, table_hbm, o_ref, kvbuf, sems):
    step = pl.program_id(0)
    steps = pl.num_programs(0)

    def fetch(block, slot):
        for j in range(TOPN):
            pltpu.make_async_copy(
                table_hbm.at[pos_ref[block * TOPN + j]], kvbuf.at[slot, j], sems.at[slot, j]
            ).start()

    @pl.when(step == 0)
    def _():
        fetch(0, 0)

    slot = step % 2

    @pl.when(step + 1 < steps)
    def _():
        fetch(step + 1, 1 - slot)

    for j in range(TOPN):
        pltpu.make_async_copy(table_hbm.at[0], kvbuf.at[slot, j], sems.at[slot, j]).wait()
    tiles = kvbuf[slot]
    k_rows = tiles[:, :, :DH].reshape(TOPN * BLOCK, DH)
    v_rows = tiles[:, :, DH:].reshape(TOPN * BLOCK, DH)
    for g in range(H // HEAD_GROUP):
        heads = range(g * HEAD_GROUP, (g + 1) * HEAD_GROUP)
        q_rows = jnp.concatenate([q_ref[:, h * DH : (h + 1) * DH] for h in heads], axis=0)
        scores = lax.dot_general(
            q_rows, k_rows, (((1,), (1,)), ((), ())), preferred_element_type=jnp.float32
        ) * DH ** (-0.5)
        weights = jnp.exp(scores - jnp.max(scores, axis=-1, keepdims=True))
        totals = jnp.sum(weights, axis=-1, keepdims=True)
        weighted = jnp.dot(
            weights.astype(jnp.bfloat16), v_rows, preferred_element_type=jnp.float32
        )
        out = (weighted / totals).astype(o_ref.dtype)
        for i, h in enumerate(heads):
            o_ref[:, h * DH : (h + 1) * DH] = out[i * QB : (i + 1) * QB]


def attend_blocks(queries, tile_table, positions):
    query_blocks = queries.shape[0] // QB
    return pl.pallas_call(
        attend_kernel,
        out_shape=jax.ShapeDtypeStruct(queries.shape, queries.dtype),
        grid_spec=pltpu.PrefetchScalarGridSpec(
            num_scalar_prefetch=1,
            grid=(query_blocks,),
            in_specs=[
                pl.BlockSpec((QB, H * DH), lambda i, pos: (i, 0)),
                pl.BlockSpec(memory_space=pl.ANY),
            ],
            out_specs=pl.BlockSpec((QB, H * DH), lambda i, pos: (i, 0)),
            scratch_shapes=[
                pltpu.VMEM((2, TOPN, BLOCK, 2 * DH), tile_table.dtype),
                pltpu.SemaphoreType.DMA((2, TOPN)),
            ],
        ),
        compiler_params=pltpu.CompilerParams(dimension_semantics=("arbitrary",)),
        cost_estimate=pl.CostEstimate(
            flops=4 * queries.shape[0] * H * TOPN * BLOCK * DH,
            transcendentals=queries.shape[0] * H * TOPN * BLOCK,
            bytes_accessed=2 * queries.size * 2 + query_blocks * TOPN * BLOCK * 2 * DH * 2,
        ),
    )(positions, queries, tile_table)


def solution(mesh):
    placed = (
        P(("pb", "kv"), None),
        P(("kv", "pb"), None),
        P(("kv", "pb"), None),
        P(("pb", "kv"), None),
    )
    return jax.shard_map(
        per_device, mesh=mesh, in_specs=placed, out_specs=P(("pb", "kv"), None), check_vma=False
    )
```
